512 devices in a mesh: sec: 2 (over y_lo), exp: 32 (over y_hi, x, core), hid: 8 (over z).
Axes of the slice: x: 4, y: 8 (y_hi: 4, y_lo: 2; y = y_hi * 2 + y_lo), z: 8, core: 2. Of those that a mesh axis runs over, the one named last changes fastest.
Arguments:
- tokens: bfloat16 [1024, 4096], P('exp', ('sec', 'hid')), may hold values from -1200 to 1200
- norm_gain: bfloat16 [4096], P(('sec', 'hid')), may hold values from 0.5 to 2
- route_weight: float32 [1024, 2], P('exp'), may hold values from 0.1 to 1
- block_experts: int32 [8, 2], replicated, may hold values from 0 to 7, all different within a row; in each aligned block of 8 rows (0 to 7, 8 to 15, ...) at most 4 rows name the same one
- w_gate: bfloat16 [2, 4096, 32768], P('sec', None, ('exp', 'hid')), may hold values from -0.09375 to 0.09375
- w_up: bfloat16 [2, 4096, 32768], P('sec', None, ('exp', 'hid')), may hold values from -0.09375 to 0.09375
- w_down: bfloat16 [2, 32768, 4096], P('sec', ('exp', 'hid')), may hold values from -0.0625 to 0.0625
Outputs:
- moe_out: bfloat16 [1024, 4096], P('exp', ('sec', 'hid'))
The draws below stay inside these ranges and needn't reach their ends.
Inputs may be any that keep to these rules, and one draw needn't show every extreme that they name: `block_experts`: each row names 2 different experts; no expert is named by more than 4 rows, a bound that some block reaches; every expert is named by some row.
All inputs are finite; a program needn't handle non-finite values.
Results may differ from the reference program's by a relative error of at most 0.018.
Values may be sent and summed in bfloat16 or wider, within the bound.
No kernel may reach another device: no remote copies, remote signals or barrier semaphores. Data moves between devices by JAX's collectives and lax.ppermute only.
A program may use at most 64 MiB of HBM per device.

```python
import math
import jax
import jax.numpy as jnp
import numpy as np
from jax import lax

D = 4096
FF = 8192
EXPERTS = 8
TOP = 2
BLK = 128
BLOCKS = 8
TOKENS = 1024
MOST = 4
FFD = 128
N_SEC = 2


def draw_tokens(key, part):
    key_rows = jax.random.fold_in(key, 11)
    key_cols = jax.random.fold_in(key, 12)
    key_base = jax.random.fold_in(key, 13)
    row_scale = jnp.exp(jax.random.uniform(key_rows, (TOKENS, 1), jnp.float32) * math.log(10.0))
    ramp = 1.0 + 2.0 * jnp.arange(D, dtype=jnp.float32)[None, :] / (D - 1)
    col_scale = jnp.exp(jax.random.uniform(key_cols, (1, D), jnp.float32) * math.log(10.0)) * ramp
    base_vals = jax.random.truncated_normal(key_base, -4.0, 4.0, (TOKENS, D), jnp.float32)
    return (row_scale * col_scale * base_vals).astype(jnp.bfloat16)


def block_scale(key, dims, shards, smallest, largest):
    gain, own = 1.0, jax.random.fold_in(key, 6)
    for position, parts in shards:
        steps = jnp.exp(jax.random.uniform(jax.random.fold_in(own, position), (parts,), jnp.float32, smallest / len(shards), largest / len(shards)))
        gain = gain * jnp.repeat(steps, dims[position] // parts).reshape([-1 if axis == position else 1 for axis in range(len(dims))])
    return gain


def routed_block(key, own, number, rows, number_of, top, reach, lean):
    sequence = jax.random.permutation(key, number_of)
    heavy_load, ordinary = portions_of(number_of, rows * top, reach, lean, True), portions_of(number_of, rows * top, reach, lean, False)
    places = jnp.arange(number_of)

    def named(sizes, rotation):
        used = int((sizes > 0).sum())
        fixed = max(1, used // 4)
        moved = fixed + (places - fixed + rotation * (used - fixed)) % max(1, number_of - fixed)
        return jnp.zeros((number_of,), jnp.int32).at[sequence[jnp.where(places < fixed, places, moved)]].set(jnp.asarray(sizes, jnp.int32))

    sizes = jnp.where(number % 4 == 0, named(heavy_load, number // 4), named(ordinary, number - number // 4 - 1))
    mixed = jax.random.permutation(jax.random.fold_in(own, 3), number_of)
    donor, taker = mixed[0:number_of // 2 * 2:2], mixed[1:number_of // 2 * 2:2]
    slack = jnp.minimum(sizes[donor] - 1, reach - sizes[taker]) // 2
    slack = jnp.where((donor == sequence[0]) | (taker == sequence[0]) | (sizes[taker] == 0), 0, jnp.maximum(slack, 0))
    moved = jax.random.randint(jax.random.fold_in(own, 4), (number_of // 2,), 0, 1 << 20) % (slack + 1)
    sizes = sizes.at[donor].add(-moved).at[taker].add(moved)
    labels = jnp.searchsorted(jnp.cumsum(sizes), jnp.arange(rows * top), side="right").astype(jnp.int32)
    table = labels.reshape(top, rows).T
    table = table[jax.random.permutation(jax.random.fold_in(own, 1), rows)]
    rotation = jax.random.randint(jax.random.fold_in(own, 2), (rows, 1), 0, top)
    return jnp.take_along_axis(table, (jnp.arange(top)[None, :] + rotation) % top, axis=1)


def portions_of(count, total, reach, lean, full):
    weights = [(1 << 20) // math.isqrt(rank ** lean) + 1 for rank in range(1, count + 1)]
    largest = reach if full else min(reach, max(-(-total // count), total * weights[0] // sum(weights)))
    least = 1 if total - largest >= count - 1 else 0
    counts, rest = [largest] + [least] * (count - 1), total - largest - least * (count - 1)
    while rest > 0:
        candidates = [i for i in range(1, count) if counts[i] < largest] or [i for i in range(1, count) if counts[i] < reach]
        pool, remaining = sum([weights[i] for i in candidates]), rest
        for i in candidates:
            more = min(reach - counts[i], max(1, remaining * weights[i] // pool), rest)
            counts[i] = counts[i] + more
            rest = rest - more
    return np.array(counts)


def scatter_about(rng, shape, width, reach, split=(), kind=jnp.bfloat16):
    values = width * jax.random.normal(rng, shape, jnp.float32)
    if split:
        values = values * block_scale(rng, shape, split, -0.22, 0.18)
    return jnp.clip(values, -reach, reach).astype(kind)


def setup_inputs(seed: int = 0) -> dict:
    key_list = jax.random.split(jax.random.key(seed), 8)
    tokens = draw_tokens(jax.random.fold_in(key_list[7], 71), 0)
    norm_gain = jnp.clip(jnp.exp(math.log(2.0) - 1.3862944 * jax.random.uniform(key_list[1], (D,), jnp.float32) ** block_scale(key_list[1], (D,), ((0, 16),), -0.2, 0.2)), 0.5, 2.0).astype(jnp.bfloat16)
    route_weight = jnp.clip(jnp.exp(math.log(1.0) - 2.3025851 * jax.random.uniform(key_list[2], (TOKENS, TOP), jnp.float32) ** block_scale(key_list[2], (TOKENS, TOP), ((0, 32),), -0.2, 0.2)), 0.1, 1.0)
    block_experts_keys = jax.random.split(jax.random.fold_in(key_list[3], 1), BLOCKS // BLOCKS)
    block_experts_turns = jax.random.permutation(jax.random.fold_in(key_list[3], 3), BLOCKS // BLOCKS)
    block_experts = jax.vmap(lambda own, number: routed_block(jax.random.fold_in(key_list[3], 2), own, number, BLOCKS, EXPERTS, TOP, MOST, 2))(block_experts_keys, block_experts_turns).reshape((BLOCKS, TOP))
    w_gate = scatter_about(key_list[4], (N_SEC, D, EXPERTS * FF // N_SEC), D ** -0.5, 0.09375, ((0, 2), (2, 256)))
    w_up = scatter_about(key_list[5], (N_SEC, D, EXPERTS * FF // N_SEC), D ** -0.5, 0.09375, ((0, 2), (2, 256)))
    w_down = scatter_about(key_list[6], (N_SEC, EXPERTS * FF // N_SEC, D), FF ** -0.5, 0.0625, ((0, 2), (1, 256)))
    return {"tokens": tokens, "norm_gain": norm_gain, "route_weight": route_weight, "block_experts": block_experts, "w_gate": w_gate, "w_up": w_up, "w_down": w_down}


def reference(tokens, norm_gain, route_weight, block_experts, w_gate, w_up, w_down):
    values = tokens.astype(jnp.float32)
    rms_value = jnp.sqrt(lax.optimization_barrier(jnp.mean(values * values, axis=1, keepdims=True)) + 1e-05)
    normed = (values * norm_gain.astype(jnp.float32) / rms_value).astype(jnp.bfloat16)
    slab_width = FF // N_SEC
    group_count = FF // FFD

    def advance(running, assignment):
        block_id = assignment // TOP
        which_pick = assignment % TOP
        expert_id = block_experts[block_id, which_pick]
        first_col = (expert_id * slab_width).astype(jnp.int32)
        gate_cols = jnp.concatenate([lax.dynamic_slice_in_dim(w_gate[section], first_col, slab_width, 1) for section in range(N_SEC)], axis=1)
        up_cols = jnp.concatenate([lax.dynamic_slice_in_dim(w_up[section], first_col, slab_width, 1) for section in range(N_SEC)], axis=1)
        down_rows = jnp.concatenate([lax.dynamic_slice_in_dim(w_down[section], first_col, slab_width, 0) for section in range(N_SEC)], axis=0)
        first_row = (block_id * BLK).astype(jnp.int32)
        block_rows = lax.dynamic_slice_in_dim(normed, first_row, BLK, 0)
        gate_acc = jnp.dot(block_rows, gate_cols, preferred_element_type=jnp.float32)
        up_acc = jnp.dot(block_rows, up_cols, preferred_element_type=jnp.float32)
        activated = (jax.nn.silu(gate_acc) * up_acc).astype(jnp.bfloat16)
        grouped = jnp.einsum('tgf,gfd->gtd', activated.reshape(BLK, group_count, FFD).astype(jnp.float32), down_rows.reshape(group_count, FFD, D).astype(jnp.float32))
        rounded = lax.optimization_barrier(grouped.astype(jnp.bfloat16)).astype(jnp.float32)
        summed = lax.optimization_barrier(jnp.sum(rounded, axis=0))
        weight_col = lax.dynamic_slice(route_weight, (first_row, which_pick.astype(jnp.int32)), (BLK, 1))
        current = lax.dynamic_slice_in_dim(running, first_row, BLK, 0)
        running = lax.dynamic_update_slice_in_dim(running, current + weight_col * summed, first_row, 0)
        return (running, None)
    running, unused = lax.scan(advance, jnp.zeros((TOKENS, D), jnp.float32), jnp.arange(BLOCKS * TOP, dtype=jnp.int32))
    return running.astype(jnp.bfloat16)
```

```python
import jax
import jax.numpy as jnp
from jax import lax
from jax.experimental import pallas as pl
from jax.experimental.pallas import tpu as pltpu
from jax.sharding import Mesh, PartitionSpec as P

EXPERTS = 8
BLK = 128
MOST = 4
F32 = jnp.float32
BF16 = jnp.bfloat16

GROUP = ("group",)
SQUARE = ("sec", "xlo")


def prep_kernel(x_ref, out_ref):
    n, rows, w = x_ref.shape
    rows -= 8
    copies = out_ref.shape[0]
    total = jnp.zeros((rows, w), F32)
    for z in range(n):
        x = x_ref[z, 0:rows, :].astype(F32)
        g = x_ref[z, rows : rows + 1, :].astype(F32)
        total = total + x * x
        y = (x * g).astype(BF16)
        for j in range(copies):
            out_ref[j, z * rows : (z + 1) * rows, :] = y
    col = jnp.sum(total, axis=1, keepdims=True)
    row = jnp.transpose(jnp.broadcast_to(col, (rows, rows)))[0:8, :]
    hi = row.astype(BF16).astype(F32)
    mid = (row - hi).astype(BF16).astype(F32)
    low = row - hi - mid
    which = lax.broadcasted_iota(jnp.int32, (8, rows), 0)
    parts = jnp.where(which == 0, hi, jnp.where(which == 1, mid, jnp.where(which == 2, low, 0.0)))
    parts = jnp.concatenate([parts, jnp.zeros((8, w - rows), F32)], axis=1).astype(BF16)
    for j in range(copies):
        out_ref[j, n * rows : n * rows + 8, :] = parts


def expert_kernel(x_ref, g0_ref, u0_ref, d0_ref, g1_ref, u1_ref, d1_ref, out_ref):
    _, tall, w = x_ref.shape
    rows = 128
    n = tall // rows
    features = 2 * n * w
    halves = []
    scales = []
    for x in range(2):
        pieces = [x_ref[2 * s + x, z * rows : (z + 1) * rows, :] for s in range(2) for z in range(n)]
        halves.append(jnp.concatenate(pieces, axis=1))
        parts = [x_ref[2 * s + x, n * rows : n * rows + 8, 0:rows].astype(F32) for s in range(2)]
        both = parts[0] + parts[1]
        total = both[0:1, :] + both[1:2, :] + both[2:3, :]
        inv = 1.0 / jnp.sqrt(total / features + 1e-05)
        scales.append(jnp.transpose(jnp.broadcast_to(inv, (rows, rows))))
    xs = jnp.concatenate(halves, axis=0)
    scale = jnp.concatenate(scales, axis=0)
    acts = []
    for g_ref, u_ref in ((g0_ref, u0_ref), (g1_ref, u1_ref)):
        acc = jnp.dot(xs, jnp.concatenate([g_ref[...], u_ref[...]], axis=1), preferred_element_type=F32)
        gate = acc[:, 0:rows] * scale
        up = acc[:, rows:] * scale
        acts.append((gate / (1.0 + jnp.exp(-gate)) * up).astype(BF16))
    act = jnp.concatenate(acts, axis=1)
    for s in range(2):
        for z in range(n):
            col = (s * n + z) * w
            down = jnp.concatenate([d0_ref[:, col : col + w], d1_ref[:, col : col + w]], axis=0)
            res = jnp.dot(act, down, preferred_element_type=F32).astype(BF16)
            for x in range(2):
                out_ref[2 * s + x, z * rows : (z + 1) * rows, :] = res[x * rows : (x + 1) * rows]


VM = pl.BlockSpec(memory_space=pltpu.VMEM)


def per_device(tokens, norm_gain, route_weight, block_experts, w_gate, w_up, w_down):
    rows, w = tokens.shape
    groups = lax.axis_size("group")
    n_hid = lax.axis_size("hid")
    me = lax.axis_index("group")
    gate0, up0, down0 = w_gate[0], w_up[0], w_down[0]
    swap = [(0, 1), (1, 0)]
    gate1 = lax.ppermute(gate0, "core", swap)
    up1 = lax.ppermute(up0, "core", swap)
    down1 = lax.ppermute(down0, "core", swap)

    hit = jnp.any(block_experts == me, axis=1)
    slot_of_block = jnp.maximum(jnp.cumsum(hit.astype(jnp.int32)) - 1, 0)
    slot_ids = jnp.arange(MOST, dtype=jnp.int32)
    match = (slot_of_block[None, :] == slot_ids[:, None]) & hit[None, :]
    block_of_slot = jnp.sum(jnp.where(match, jnp.arange(groups, dtype=jnp.int32)[None, :], 0), axis=1)

    blocks = lax.all_to_all(
        jnp.broadcast_to(tokens[None], (groups, rows, w)), GROUP, split_axis=0, concat_axis=0, tiled=True
    )
    picked = jnp.take(blocks, block_of_slot, axis=0, mode="clip").reshape(MOST * rows, w)
    picked = jnp.concatenate([picked, jnp.broadcast_to(norm_gain[None, :], (8, w))], axis=0)
    tall = MOST * rows
    wide = lax.all_to_all(
        jnp.broadcast_to(picked[None], (n_hid, tall + 8, w)), "hid", split_axis=0, concat_axis=0, tiled=True
    )
    ready = pl.pallas_call(
        prep_kernel,
        out_shape=jax.ShapeDtypeStruct((4, n_hid * tall + 8, w), BF16),
        in_specs=[VM],
        out_specs=VM,
        name="prep",
    )(wide)
    every = lax.all_to_all(ready, SQUARE, split_axis=0, concat_axis=0, tiled=True)
    partial = pl.pallas_call(
        expert_kernel,
        out_shape=jax.ShapeDtypeStruct((4, n_hid * tall, w), BF16),
        in_specs=[VM] * 7,
        out_specs=VM,
        name="expert",
    )(every, gate0, up0, down0, gate1, up1, down1)
    got = lax.all_to_all(partial, SQUARE, split_axis=0, concat_axis=0, tiled=True)
    summed = jnp.sum(got.astype(F32), axis=0).astype(BF16).reshape(n_hid, tall, w)
    got = lax.all_to_all(summed, "hid", split_axis=0, concat_axis=0, tiled=True)
    summed = jnp.sum(got.astype(F32), axis=0).astype(BF16).reshape(MOST, rows, w)
    outgoing = jnp.take(summed, slot_of_block, axis=0, mode="clip")
    back = lax.all_to_all(outgoing, GROUP, split_axis=0, concat_axis=0, tiled=True)
    mine = jnp.take(block_experts, me, axis=0, mode="clip")
    chosen = jnp.take(back, mine, axis=0, mode="clip").astype(F32)
    result = route_weight[:, 0:1] * chosen[0] + route_weight[:, 1:2] * chosen[1]
    return result.astype(BF16)


def solution(mesh):
    devices = mesh.devices.reshape(2, EXPERTS, 2, 2, 8)
    fine = Mesh(devices, ("sec", "group", "xlo", "core", "hid"))
    exp = ("group", "xlo", "core")
    return jax.shard_map(
        per_device,
        mesh=fine,
        in_specs=(
            P(exp, ("sec", "hid")),
            P(("sec", "hid")),
            P(exp, None),
            P(),
            P("sec", None, exp + ("hid",)),
            P("sec", None, exp + ("hid",)),
            P("sec", exp + ("hid",), None),
        ),
        out_specs=P(exp, ("sec", "hid")),
        check_vma=False,
    )
```

```python
import jax
import jax.numpy as jnp
from jax import lax
from jax.experimental import pallas as pl
from jax.experimental.pallas import tpu as pltpu
from jax.sharding import Mesh, PartitionSpec as P


EXPERTS = 8
MOST = 4
HID = 8
F32 = jnp.float32
BF16 = jnp.bfloat16

GROUP = ("group",)
SQUARE = ("sec", "xlo")


def prep_kernel(x_ref, out_ref, y_ref, sems):
    n, rows, w = x_ref.shape
    rows -= 8
    copies = out_ref.shape[0]
    total = jnp.zeros((rows, w), F32)
    for z in range(n):
        x = x_ref[z, 0:rows, :].astype(F32)
        g = x_ref[z, rows : rows + 1, :].astype(F32)
        total = total + x * x
        y_ref[z * rows : (z + 1) * rows, :] = (x * g).astype(BF16)
    col = jnp.sum(total, axis=1, keepdims=True)
    row = jnp.transpose(jnp.broadcast_to(col, (rows, rows)))[0:8, :]
    hi = row.astype(BF16).astype(F32)
    mid = (row - hi).astype(BF16).astype(F32)
    low = row - hi - mid
    which = lax.broadcasted_iota(jnp.int32, (8, rows), 0)
    parts = jnp.where(which == 0, hi, jnp.where(which == 1, mid, jnp.where(which == 2, low, 0.0)))
    y_ref[n * rows : n * rows + 8, :] = jnp.concatenate([parts, jnp.zeros((8, w - rows), F32)], axis=1).astype(BF16)
    sends = [pltpu.make_async_copy(y_ref, out_ref.at[j], sems.at[j]) for j in range(copies)]
    for send in sends:
        send.start()
    for send in sends:
        send.wait()


def gate_up_kernel(x_ref, g0, u0, g1, u1, act_ref, w_ref, sems):
    _, tall, w = x_ref.shape
    n = HID
    rows = (tall - 8) // n
    depth = n * w
    ff = g0.shape[1]
    loads = []
    for s in range(2):
        for c, pair in enumerate(((g0, u0), (g1, u1))):
            for k, ref in enumerate(pair):
                loads.append(
                    pltpu.make_async_copy(
                        ref.at[s * depth : (s + 1) * depth, :],
                        w_ref.at[c, s * depth : (s + 1) * depth, k * ff : (k + 1) * ff],
                        sems.at[len(loads)],
                    )
                )
    for load in loads:
        load.start()
    scales = []
    for x in range(2):
        parts = [x_ref[2 * s + x, n * rows : n * rows + 8, 0:rows].astype(F32) for s in range(2)]
        both = parts[0] + parts[1]
        total = both[0:1, :] + both[1:2, :] + both[2:3, :]
        inv = 1.0 / jnp.sqrt(total / (2 * depth) + 1e-05)
        scales.append(jnp.transpose(jnp.broadcast_to(inv, (rows, rows))))
    scale = jnp.concatenate(scales, axis=0)
    accs = [None, None]
    for s in range(2):
        xs = jnp.concatenate(
            [
                jnp.concatenate([x_ref[2 * s + x, z * rows : (z + 1) * rows, :] for z in range(n)], axis=1)
                for x in range(2)
            ],
            axis=0,
        )
        for c in range(2):
            loads[4 * s + 2 * c].wait()
            loads[4 * s + 2 * c + 1].wait()
            part = jnp.dot(xs, w_ref[c, s * depth : (s + 1) * depth, :], preferred_element_type=F32)
            accs[c] = part if accs[c] is None else accs[c] + part
    for c, acc in enumerate(accs):
        gate = acc[:, 0:ff] * scale
        up = acc[:, ff:] * scale
        act = (gate / (1.0 + jnp.exp(-gate)) * up).astype(BF16)
        for s in range(2):
            for x in range(2):
                act_ref[2 * s + x, :, c * ff : (c + 1) * ff] = act[x * rows : (x + 1) * rows]


def down_kernel(where_ref, act_ref, *refs):
    *downs, out_ref, w_ref, sems = refs
    n, _, w = out_ref.shape
    ff = downs[0].shape[0]
    half = n * w // 2
    loads = []
    for h in range(2):
        for i, ref in enumerate(downs):
            loads.append(
                pltpu.make_async_copy(
                    ref.at[:, h * half : (h + 1) * half],
                    w_ref.at[i * ff : (i + 1) * ff, h * half : (h + 1) * half],
                    sems.at[len(loads)],
                )
            )
    for load in loads:
        load.start()
    act = jnp.concatenate([act_ref[where_ref[k]] for k in range(4)], axis=1)
    for h in range(2):
        for load in loads[8 * h : 8 * h + 8]:
            load.wait()
        for z in range(h * n // 2, (h + 1) * n // 2):
            out_ref[z] = jnp.dot(act, w_ref[:, z * w : (z + 1) * w], preferred_element_type=F32).astype(BF16)


VM = pl.BlockSpec(memory_space=pltpu.VMEM)
SM = pl.BlockSpec(memory_space=pltpu.SMEM)
ANY = pl.BlockSpec(memory_space=pl.ANY)


def vm(x):
    return pltpu.with_memory_space_constraint(x, pltpu.VMEM)


def prepared(x):
    n, rows, w = x.shape
    tall = n * (rows - 8) + 8
    return pl.pallas_call(
        prep_kernel,
        out_shape=pltpu.HBM((4, tall, w), BF16),
        in_specs=[VM],
        out_specs=ANY,
        scratch_shapes=[pltpu.VMEM((tall, w), BF16), pltpu.SemaphoreType.DMA((4,))],
        compiler_params=pltpu.CompilerParams(vmem_limit_bytes=4 << 20),
        name="prep",
    )(vm(x))


def gated(x, weights):
    _, tall, _ = x.shape
    deep, ff = weights[0].shape
    return pl.pallas_call(
        gate_up_kernel,
        out_shape=jax.ShapeDtypeStruct((4, (tall - 8) // HID, 2 * ff), BF16),
        in_specs=[VM] + [ANY] * 4,
        out_specs=VM,
        scratch_shapes=[pltpu.VMEM((2, deep, 2 * ff), BF16), pltpu.SemaphoreType.DMA((8,))],
        compiler_params=pltpu.CompilerParams(vmem_limit_bytes=16 << 20),
        name="gate_up",
    )(vm(x), *weights)


def lowered(where, act, downs):
    _, rows, _ = act.shape
    ff, wide = downs[0].shape
    return pl.pallas_call(
        down_kernel,
        out_shape=jax.ShapeDtypeStruct((HID, rows, wide // HID), BF16),
        in_specs=[SM, VM] + [ANY] * 8,
        out_specs=VM,
        scratch_shapes=[pltpu.VMEM((8 * ff, wide), BF16), pltpu.SemaphoreType.DMA((16,))],
        compiler_params=pltpu.CompilerParams(vmem_limit_bytes=16 << 20),
        name="down",
    )(where, vm(act), *downs)


def exchange(x, axes):
    return lax.all_to_all(x, axes, split_axis=0, concat_axis=0, tiled=True)


def added(x):
    return jnp.sum(x.astype(F32), axis=0).astype(BF16)


def shifted(x, flip):
    return lax.ppermute(x, SQUARE, [(i, i ^ flip) for i in range(4)])


def layer(tokens, norm_gain, route_weight, block_experts, w_gate, w_up, w_down):
    rows, w = tokens.shape
    groups = lax.axis_size("group")
    n_hid = lax.axis_size("hid")
    me = lax.axis_index("group")
    gate0, up0, down0 = w_gate[0], w_up[0], w_down[0]
    sec = lax.axis_index("sec")
    place = sec * 2 + lax.axis_index("xlo")
    part = down0.shape[1] // 2
    down_here = lax.dynamic_slice_in_dim(down0, sec * part, part, 1)
    down_away = lax.dynamic_slice_in_dim(down0, (1 - sec) * part, part, 1)
    direct = [down_here]
    for flip, source in ((1, down_here), (2, down_away), (3, down_away)):
        direct.append(shifted(source, flip))

    def swapped(x):
        return lax.ppermute(x, "core", [(0, 1), (1, 0)])

    gate1, up1 = swapped(gate0), swapped(up0)
    downs = [d for piece in direct for d in (piece, swapped(piece))]
    where = place ^ jnp.arange(4, dtype=jnp.int32)

    hit = jnp.any(block_experts == me, axis=1)
    slot_of_block = jnp.maximum(jnp.cumsum(hit.astype(jnp.int32)) - 1, 0)
    slot_ids = jnp.arange(MOST, dtype=jnp.int32)
    match = (slot_of_block[None, :] == slot_ids[:, None]) & hit[None, :]
    block_of_slot = jnp.sum(jnp.where(match, jnp.arange(groups, dtype=jnp.int32)[None, :], 0), axis=1)

    mine = jnp.take(block_experts, me, axis=0, mode="clip")
    named = mine[None, :] == jnp.arange(EXPERTS, dtype=jnp.int32)[:, None]
    factor = jnp.sum(jnp.where(named[:, None, :], route_weight[None], 0.0), axis=2)

    blocks = exchange(jnp.broadcast_to(tokens[None], (groups, rows, w)), GROUP)
    tall = MOST * rows
    picked = jnp.take(blocks, block_of_slot, axis=0, mode="clip").reshape(tall, w)
    picked = jnp.concatenate([picked, jnp.broadcast_to(norm_gain[None, :], (8, w))], axis=0)
    wide = exchange(jnp.broadcast_to(picked[None], (n_hid, tall + 8, w)), "hid")
    every = exchange(prepared(wide), SQUARE)
    act = exchange(gated(every, (gate0, up0, gate1, up1)), SQUARE)
    summed = added(exchange(lowered(where, act, downs), "hid")).reshape(MOST, rows, w)
    outgoing = jnp.take(summed, slot_of_block, axis=0, mode="clip")
    back = exchange(outgoing, GROUP)
    return jnp.sum(back.astype(F32) * factor[:, :, None], axis=0).astype(BF16)


def solution(mesh):
    devices = mesh.devices.reshape(2, EXPERTS, 2, 2, 8)
    fine = Mesh(devices, ("sec", "group", "xlo", "core", "hid"))
    exp = ("group", "xlo", "core")
    return jax.shard_map(
        layer,
        mesh=fine,
        in_specs=(
            P(exp, ("sec", "hid")),
            P(("sec", "hid")),
            P(exp, None),
            P(),
            P("sec", None, exp + ("hid",)),
            P("sec", None, exp + ("hid",)),
            P("sec", exp + ("hid",), None),
        ),
        out_specs=P(exp, ("sec", "hid")),
        check_vma=False,
    )
```

```python
import jax
import jax.numpy as jnp
from jax import lax
from jax.experimental import pallas as pl
from jax.experimental.pallas import tpu as pltpu
from jax.sharding import Mesh, PartitionSpec as P


EXPERTS = 8
MOST = 4
HID = 8
F32 = jnp.float32
BF16 = jnp.bfloat16

GROUP = ("group",)
SQUARE = ("sec", "xlo")


def prep_kernel(x_ref, out_ref, y_ref, sems):
    n, rows, w = x_ref.shape
    rows -= 8
    copies = out_ref.shape[0]
    total = jnp.zeros((rows, w), F32)
    for z in range(n):
        x = x_ref[z, 0:rows, :].astype(F32)
        g = x_ref[z, rows : rows + 1, :].astype(F32)
        total = total + x * x
        y_ref[z * rows : (z + 1) * rows, :] = (x * g).astype(BF16)
    col = jnp.sum(total, axis=1, keepdims=True)
    row = jnp.transpose(jnp.broadcast_to(col, (rows, rows)))[0:8, :]
    hi = row.astype(BF16).astype(F32)
    mid = (row - hi).astype(BF16).astype(F32)
    low = row - hi - mid
    which = lax.broadcasted_iota(jnp.int32, (8, rows), 0)
    parts = jnp.where(which == 0, hi, jnp.where(which == 1, mid, jnp.where(which == 2, low, 0.0)))
    y_ref[n * rows : n * rows + 8, :] = jnp.concatenate([parts, jnp.zeros((8, w - rows), F32)], axis=1).astype(BF16)
    sends = [pltpu.make_async_copy(y_ref, out_ref.at[j], sems.at[j]) for j in range(copies)]
    for send in sends:
        send.start()
    for send in sends:
        send.wait()


def gate_up_kernel(x_ref, g0, u0, g1, u1, act_ref, w_ref, sems):
    _, tall, w = x_ref.shape
    n = HID
    rows = (tall - 8) // n
    depth = n * w
    ff = g0.shape[1]
    loads = []
    for s in range(2):
        for c, pair in enumerate(((g0, u0), (g1, u1))):
            for k, ref in enumerate(pair):
                loads.append(
                    pltpu.make_async_copy(
                        ref.at[s * depth : (s + 1) * depth, :],
                        w_ref.at[c, s * depth : (s + 1) * depth, k * ff : (k + 1) * ff],
                        sems.at[len(loads)],
                    )
                )
    for load in loads:
        load.start()
    scales = []
    for x in range(2):
        parts = [x_ref[2 * s + x, n * rows : n * rows + 8, 0:rows].astype(F32) for s in range(2)]
        both = parts[0] + parts[1]
        total = both[0:1, :] + both[1:2, :] + both[2:3, :]
        inv = 1.0 / jnp.sqrt(total / (2 * depth) + 1e-05)
        scales.append(jnp.transpose(jnp.broadcast_to(inv, (rows, rows))))
    scale = jnp.concatenate(scales, axis=0)
    accs = [None, None]
    for s in range(2):
        xs = jnp.concatenate(
            [
                jnp.concatenate([x_ref[2 * s + x, z * rows : (z + 1) * rows, :] for z in range(n)], axis=1)
                for x in range(2)
            ],
            axis=0,
        )
        for c in range(2):
            loads[4 * s + 2 * c].wait()
            loads[4 * s + 2 * c + 1].wait()
            part = jnp.dot(xs, w_ref[c, s * depth : (s + 1) * depth, :], preferred_element_type=F32)
            accs[c] = part if accs[c] is None else accs[c] + part
    for c, acc in enumerate(accs):
        gate = acc[:, 0:ff] * scale
        up = acc[:, ff:] * scale
        act = (gate / (1.0 + jnp.exp(-gate)) * up).astype(BF16)
        for s in range(2):
            for x in range(2):
                act_ref[2 * s + x, :, c * ff : (c + 1) * ff] = act[x * rows : (x + 1) * rows]


def down_kernel(where_ref, act_ref, *refs):
    *downs, out_ref, w_ref, sems = refs
    n, _, w = out_ref.shape
    ff = downs[0].shape[0]
    half = n * w // 2
    loads = []
    for h in range(2):
        for i, ref in enumerate(downs):
            loads.append(
                pltpu.make_async_copy(
                    ref.at[:, h * half : (h + 1) * half],
                    w_ref.at[i * ff : (i + 1) * ff, h * half : (h + 1) * half],
                    sems.at[len(loads)],
                )
            )
    for load in loads:
        load.start()
    act = jnp.concatenate([act_ref[where_ref[k]] for k in range(4)], axis=1)
    for h in range(2):
        for load in loads[8 * h : 8 * h + 8]:
            load.wait()
        for z in range(h * n // 2, (h + 1) * n // 2):
            out_ref[z] = jnp.dot(act, w_ref[:, z * w : (z + 1) * w], preferred_element_type=F32).astype(BF16)


VM = pl.BlockSpec(memory_space=pltpu.VMEM)
SM = pl.BlockSpec(memory_space=pltpu.SMEM)
HBM = pl.BlockSpec(memory_space=pltpu.HBM)


def vm(x):
    return pltpu.with_memory_space_constraint(x, pltpu.VMEM)


def hbm(x):
    return pltpu.with_memory_space_constraint(x, pltpu.HBM)


def prepared(x):
    n, rows, w = x.shape
    tall = n * (rows - 8) + 8
    return pl.pallas_call(
        prep_kernel,
        out_shape=pltpu.HBM((4, tall, w), BF16),
        in_specs=[VM],
        out_specs=HBM,
        scratch_shapes=[pltpu.VMEM((tall, w), BF16), pltpu.SemaphoreType.DMA((4,))],
        compiler_params=pltpu.CompilerParams(vmem_limit_bytes=4 << 20),
        name="prep",
    )(vm(x))


def gated(x, weights):
    _, tall, _ = x.shape
    deep, ff = weights[0].shape
    return pl.pallas_call(
        gate_up_kernel,
        out_shape=jax.ShapeDtypeStruct((4, (tall - 8) // HID, 2 * ff), BF16),
        in_specs=[VM] + [HBM] * 4,
        out_specs=VM,
        scratch_shapes=[pltpu.VMEM((2, deep, 2 * ff), BF16), pltpu.SemaphoreType.DMA((8,))],
        compiler_params=pltpu.CompilerParams(vmem_limit_bytes=16 << 20),
        name="gate_up",
    )(vm(x), *[hbm(v) for v in weights])


def lowered(where, act, downs):
    _, rows, _ = act.shape
    ff, wide = downs[0].shape
    return pl.pallas_call(
        down_kernel,
        out_shape=jax.ShapeDtypeStruct((HID, rows, wide // HID), BF16),
        in_specs=[SM, VM] + [HBM] * 8,
        out_specs=VM,
        scratch_shapes=[pltpu.VMEM((8 * ff, wide), BF16), pltpu.SemaphoreType.DMA((16,))],
        compiler_params=pltpu.CompilerParams(vmem_limit_bytes=16 << 20),
        name="down",
    )(where, vm(act), *[hbm(v) for v in downs])


def exchange(x, axes):
    return lax.all_to_all(x, axes, split_axis=0, concat_axis=0, tiled=True)


def added(x):
    return jnp.sum(x.astype(F32), axis=0).astype(BF16)


def shifted(x, flip):
    return lax.ppermute(x, SQUARE, [(i, i ^ flip) for i in range(4)])


def layer(tokens, norm_gain, route_weight, block_experts, w_gate, w_up, w_down):
    rows, w = tokens.shape
    groups = lax.axis_size("group")
    n_hid = lax.axis_size("hid")
    me = lax.axis_index("group")
    gate0, up0, down0 = w_gate[0], w_up[0], w_down[0]
    sec = lax.axis_index("sec")
    place = sec * 2 + lax.axis_index("xlo")
    part = down0.shape[1] // 2
    down_here = lax.dynamic_slice_in_dim(down0, sec * part, part, 1)
    down_away = lax.dynamic_slice_in_dim(down0, (1 - sec) * part, part, 1)
    direct = [down_here]
    for flip, source in ((1, down_here), (2, down_away), (3, down_away)):
        direct.append(shifted(source, flip))

    def swapped(x):
        return lax.ppermute(x, "core", [(0, 1), (1, 0)])

    gate1, up1 = swapped(gate0), swapped(up0)
    downs = [d for piece in direct for d in (piece, swapped(piece))]
    where = place ^ jnp.arange(4, dtype=jnp.int32)

    hit = jnp.any(block_experts == me, axis=1)
    slot_of_block = jnp.maximum(jnp.cumsum(hit.astype(jnp.int32)) - 1, 0)
    slot_ids = jnp.arange(MOST, dtype=jnp.int32)
    match = (slot_of_block[None, :] == slot_ids[:, None]) & hit[None, :]
    block_of_slot = jnp.sum(jnp.where(match, jnp.arange(groups, dtype=jnp.int32)[None, :], 0), axis=1)

    mine = jnp.take(block_experts, me, axis=0, mode="clip")
    named = mine[None, :] == jnp.arange(EXPERTS, dtype=jnp.int32)[:, None]
    factor = jnp.sum(jnp.where(named[:, None, :], route_weight[None], 0.0), axis=2)

    blocks = exchange(jnp.broadcast_to(tokens[None], (groups, rows, w)), GROUP)
    tall = MOST * rows
    picked = jnp.take(blocks, block_of_slot, axis=0, mode="clip").reshape(tall, w)
    picked = jnp.concatenate([picked, jnp.broadcast_to(norm_gain[None, :], (8, w))], axis=0)
    wide = exchange(jnp.broadcast_to(picked[None], (n_hid, tall + 8, w)), "hid")
    ready = prepared(wide)
    every = exchange(ready, SQUARE)
    act = exchange(gated(every, (gate0, up0, gate1, up1)), SQUARE)
    summed = added(exchange(lowered(where, act, downs), "hid")).reshape(MOST, rows, w)
    outgoing = jnp.take(summed, slot_of_block, axis=0, mode="clip")
    back = exchange(outgoing, GROUP)
    return jnp.sum(back.astype(F32) * factor[:, :, None], axis=0).astype(BF16)


def solution(mesh):
    devices = mesh.devices.reshape(2, EXPERTS, 2, 2, 8)
    fine = Mesh(devices, ("sec", "group", "xlo", "core", "hid"))
    exp = ("group", "xlo", "core")
    return jax.shard_map(
        layer,
        mesh=fine,
        in_specs=(
            P(exp, ("sec", "hid")),
            P(("sec", "hid")),
            P(exp, None),
            P(),
            P("sec", None, exp + ("hid",)),
            P("sec", None, exp + ("hid",)),
            P("sec", exp + ("hid",), None),
        ),
        out_specs=P(exp, ("sec", "hid")),
        check_vma=False,
    )
```

```python
import jax
import jax.numpy as jnp
from jax import lax
from jax.experimental import pallas as pl
from jax.experimental.pallas import tpu as pltpu
from jax.sharding import Mesh, PartitionSpec as P


EXPERTS = 8
MOST = 4
HID = 8
F32 = jnp.float32
BF16 = jnp.bfloat16

GROUP = ("group",)
SQUARE = ("sec", "xlo")


def prep_kernel(x_ref, out_ref, y_ref, sems):
    n, rows, w = x_ref.shape
    rows -= 8
    copies = out_ref.shape[0]
    total = jnp.zeros((rows, w), F32)
    for z in range(n):
        x = x_ref[z, 0:rows, :].astype(F32)
        g = x_ref[z, rows : rows + 1, :].astype(F32)
        total = total + x * x
        y_ref[z * rows : (z + 1) * rows, :] = (x * g).astype(BF16)
    col = jnp.sum(total, axis=1, keepdims=True)
    row = jnp.transpose(jnp.broadcast_to(col, (rows, rows)))[0:8, :]
    hi = row.astype(BF16).astype(F32)
    mid = (row - hi).astype(BF16).astype(F32)
    low = row - hi - mid
    which = lax.broadcasted_iota(jnp.int32, (8, rows), 0)
    parts = jnp.where(which == 0, hi, jnp.where(which == 1, mid, jnp.where(which == 2, low, 0.0)))
    y_ref[n * rows : n * rows + 8, :] = jnp.concatenate([parts, jnp.zeros((8, w - rows), F32)], axis=1).astype(BF16)
    sends = [pltpu.make_async_copy(y_ref, out_ref.at[j], sems.at[j]) for j in range(copies)]
    for send in sends:
        send.start()
    for send in sends:
        send.wait()


def gate_up_kernel(x_ref, g0, u0, g1, u1, act_ref, w_ref, acc_ref, sems):
    _, tall, w = x_ref.shape
    n = HID
    rows = (tall - 8) // n
    deep, ff = g0.shape
    chunks = 4
    per = deep // chunks
    loads = [
        [
            pltpu.make_async_copy(
                ref.at[c * per : (c + 1) * per, :], w_ref.at[i, c * per : (c + 1) * per, :], sems.at[c, i]
            )
            for i, ref in enumerate((g0, u0, g1, u1))
        ]
        for c in range(chunks)
    ]
    for c in range(2):
        for load in loads[c]:
            load.start()
    scales = []
    for x in range(2):
        parts = [x_ref[2 * s + x, n * rows : n * rows + 8, 0:rows].astype(F32) for s in range(2)]
        both = parts[0] + parts[1]
        total = both[0:1, :] + both[1:2, :] + both[2:3, :]
        inv = 1.0 / jnp.sqrt(total / deep + 1e-05)
        scales.append(jnp.transpose(jnp.broadcast_to(inv, (rows, rows))))
    for c in range(chunks):
        pieces = range(c * per // w, (c + 1) * per // w)
        xs = jnp.concatenate(
            [
                jnp.concatenate(
                    [x_ref[2 * (p // n) + x, (p % n) * rows : (p % n + 1) * rows, :] for p in pieces], axis=1
                )
                for x in range(2)
            ],
            axis=0,
        )
        for load in loads[c]:
            load.wait()
        if c + 2 < chunks:
            for load in loads[c + 2]:
                load.start()
        ws = jnp.concatenate([w_ref[i, c * per : (c + 1) * per, :] for i in range(4)], axis=1)
        part = jnp.dot(xs, ws, preferred_element_type=F32)
        if c == 0:
            acc_ref[...] = part
        elif c + 1 < chunks:
            acc_ref[...] += part
        else:
            acc = acc_ref[...] + part
    for k in range(2):
        for x in range(2):
            block = acc[x * rows : (x + 1) * rows, 2 * k * ff : 2 * (k + 1) * ff]
            gate = block[:, 0:ff] * scales[x]
            up = block[:, ff:] * scales[x]
            act = (gate / (1.0 + jnp.exp(-gate)) * up).astype(BF16)
            for s in range(2):
                act_ref[2 * s + x, :, k * ff : (k + 1) * ff] = act


def down_kernel(where_ref, act_ref, *refs):
    *downs, out_ref, w_ref, sems = refs
    n, _, w = out_ref.shape
    ff = downs[0].shape[0]
    chunks = 4
    per = n * w // chunks
    loads = [
        [
            pltpu.make_async_copy(
                ref.at[:, h * per : (h + 1) * per],
                w_ref.at[i * ff : (i + 1) * ff, h * per : (h + 1) * per],
                sems.at[h, i],
            )
            for i, ref in enumerate(downs)
        ]
        for h in range(chunks)
    ]
    for h in range(2):
        for load in loads[h]:
            load.start()
    act = jnp.concatenate([act_ref[where_ref[k]] for k in range(4)], axis=1)
    for h in range(chunks):
        for load in loads[h]:
            load.wait()
        if h + 2 < chunks:
            for load in loads[h + 2]:
                load.start()
        for z in range(h * n // chunks, (h + 1) * n // chunks):
            out_ref[z] = jnp.dot(act, w_ref[:, z * w : (z + 1) * w], preferred_element_type=F32).astype(BF16)


def spread_kernel(x_ref, out_ref, sems):
    sends = [pltpu.make_async_copy(x_ref, out_ref.at[j], sems.at[j]) for j in range(out_ref.shape[0])]
    for send in sends:
        send.start()
    for send in sends:
        send.wait()


def pick_kernel(block_ref, x_ref, gain_ref, out_ref, y_ref, sems):
    _, rows, w = x_ref.shape
    for k in range(MOST):
        y_ref[k * rows : (k + 1) * rows, :] = x_ref[block_ref[k]]
    y_ref[MOST * rows : MOST * rows + 8, :] = jnp.broadcast_to(gain_ref[...].astype(F32), (8, w)).astype(BF16)
    spread_kernel(y_ref, out_ref, sems)


def home_kernel(slot_ref, x_ref, out_ref, y_ref, sems):
    _, rows, _ = out_ref.shape
    total = x_ref[0].astype(F32)
    for z in range(1, x_ref.shape[0]):
        total = total + x_ref[z].astype(F32)
    total = total.astype(BF16)
    for k in range(MOST):
        y_ref[k] = total[k * rows : (k + 1) * rows]
    sends = [pltpu.make_async_copy(y_ref.at[slot_ref[b]], out_ref.at[b], sems.at[b]) for b in range(out_ref.shape[0])]
    for send in sends:
        send.start()
    for send in sends:
        send.wait()


VM = pl.BlockSpec(memory_space=pltpu.VMEM)
SM = pl.BlockSpec(memory_space=pltpu.SMEM)
HBM = pl.BlockSpec(memory_space=pltpu.HBM)


def vm(x):
    return pltpu.with_memory_space_constraint(x, pltpu.VMEM)


def hbm(x):
    return pltpu.with_memory_space_constraint(x, pltpu.HBM)


def prepared(x):
    n, rows, w = x.shape
    tall = n * (rows - 8) + 8
    return pl.pallas_call(
        prep_kernel,
        out_shape=pltpu.HBM((4, tall, w), BF16),
        in_specs=[VM],
        out_specs=HBM,
        scratch_shapes=[pltpu.VMEM((tall, w), BF16), pltpu.SemaphoreType.DMA((4,))],
        compiler_params=pltpu.CompilerParams(vmem_limit_bytes=4 << 20),
        name="prep",
    )(vm(x))


def gated(x, weights):
    _, tall, _ = x.shape
    rows = (tall - 8) // HID
    deep, ff = weights[0].shape
    return pl.pallas_call(
        gate_up_kernel,
        out_shape=pltpu.HBM((4, rows, 2 * ff), BF16),
        in_specs=[VM] + [HBM] * 4,
        out_specs=VM,
        scratch_shapes=[
            pltpu.VMEM((4, deep, ff), BF16),
            pltpu.VMEM((2 * rows, 4 * ff), F32),
            pltpu.SemaphoreType.DMA((4, 4)),
        ],
        compiler_params=pltpu.CompilerParams(vmem_limit_bytes=16 << 20),
        name="gate_up",
    )(vm(x), *[hbm(v) for v in weights])


def lowered(where, act, downs):
    _, rows, _ = act.shape
    ff, wide = downs[0].shape
    return pl.pallas_call(
        down_kernel,
        out_shape=jax.ShapeDtypeStruct((HID, rows, wide // HID), BF16),
        in_specs=[SM, VM] + [HBM] * 8,
        out_specs=VM,
        scratch_shapes=[pltpu.VMEM((8 * ff, wide), BF16), pltpu.SemaphoreType.DMA((4, 8))],
        compiler_params=pltpu.CompilerParams(vmem_limit_bytes=16 << 20),
        name="down",
    )(where, vm(act), *[hbm(v) for v in downs])


def repeated(x, copies):
    return pl.pallas_call(
        spread_kernel,
        out_shape=pltpu.HBM((copies, *x.shape), x.dtype),
        in_specs=[HBM],
        out_specs=HBM,
        scratch_shapes=[pltpu.SemaphoreType.DMA((copies,))],
        compiler_params=pltpu.CompilerParams(vmem_limit_bytes=1 << 20),
    )(hbm(x))


def picked_rows(block_of_slot, blocks, norm_gain, copies):
    _, rows, w = blocks.shape
    tall = MOST * rows + 8
    return pl.pallas_call(
        pick_kernel,
        out_shape=pltpu.HBM((copies, tall, w), BF16),
        in_specs=[SM, VM, VM],
        out_specs=HBM,
        scratch_shapes=[pltpu.VMEM((tall, w), BF16), pltpu.SemaphoreType.DMA((copies,))],
        compiler_params=pltpu.CompilerParams(vmem_limit_bytes=1 << 20),
    )(block_of_slot, vm(blocks), norm_gain[None, :])


def homed(slot_of_block, parts):
    _, tall, w = parts.shape
    rows = tall // MOST
    return pl.pallas_call(
        home_kernel,
        out_shape=pltpu.HBM((slot_of_block.shape[0], rows, w), BF16),
        in_specs=[SM, VM],
        out_specs=HBM,
        scratch_shapes=[pltpu.VMEM((MOST, rows, w), BF16), pltpu.SemaphoreType.DMA((slot_of_block.shape[0],))],
        compiler_params=pltpu.CompilerParams(vmem_limit_bytes=2 << 20),
        name="home",
    )(slot_of_block, vm(parts))


def exchange(x, axes):
    return lax.all_to_all(x, axes, split_axis=0, concat_axis=0, tiled=True)


def shifted(x, flip):
    return lax.ppermute(x, SQUARE, [(i, i ^ flip) for i in range(4)])


def layer(tokens, norm_gain, route_weight, block_experts, w_gate, w_up, w_down):
    groups = lax.axis_size("group")
    n_hid = lax.axis_size("hid")
    me = lax.axis_index("group")
    gate0, up0, down0 = w_gate[0], w_up[0], w_down[0]
    sec = lax.axis_index("sec")
    place = sec * 2 + lax.axis_index("xlo")
    part = down0.shape[1] // 2
    down_here = lax.dynamic_slice_in_dim(down0, sec * part, part, 1)
    down_away = lax.dynamic_slice_in_dim(down0, (1 - sec) * part, part, 1)
    direct = [down_here]
    for flip, source in ((1, down_here), (2, down_away), (3, down_away)):
        direct.append(shifted(source, flip))

    def swapped(x):
        return lax.ppermute(x, "core", [(0, 1), (1, 0)])

    gate1, up1 = swapped(gate0), swapped(up0)
    downs = [d for piece in direct for d in (piece, swapped(piece))]
    where = place ^ jnp.arange(4, dtype=jnp.int32)

    hit = jnp.any(block_experts == me, axis=1)
    slot_of_block = jnp.maximum(jnp.cumsum(hit.astype(jnp.int32)) - 1, 0)
    slot_ids = jnp.arange(MOST, dtype=jnp.int32)
    match = (slot_of_block[None, :] == slot_ids[:, None]) & hit[None, :]
    block_of_slot = jnp.sum(jnp.where(match, jnp.arange(groups, dtype=jnp.int32)[None, :], 0), axis=1)

    mine = jnp.take(block_experts, me, axis=0, mode="clip")
    named = mine[None, :] == jnp.arange(EXPERTS, dtype=jnp.int32)[:, None]
    factor = jnp.sum(jnp.where(named[:, None, :], route_weight[None], 0.0), axis=2)

    blocks = exchange(repeated(tokens, groups), GROUP)
    wide = picked_rows(block_of_slot, blocks, norm_gain, n_hid)
    wide = exchange(wide, "hid")
    ready = prepared(wide)
    every = exchange(ready, SQUARE)
    act = exchange(gated(every, (gate0, up0, gate1, up1)), SQUARE)
    parts = exchange(lowered(where, act, downs), "hid")
    back = exchange(homed(slot_of_block, parts), GROUP)
    return jnp.sum(back.astype(F32) * factor[:, :, None], axis=0).astype(BF16)


def solution(mesh):
    devices = mesh.devices.reshape(2, EXPERTS, 2, 2, 8)
    fine = Mesh(devices, ("sec", "group", "xlo", "core", "hid"))
    exp = ("group", "xlo", "core")
    return jax.shard_map(
        layer,
        mesh=fine,
        in_specs=(
            P(exp, ("sec", "hid")),
            P(("sec", "hid")),
            P(exp, None),
            P(),
            P("sec", None, exp + ("hid",)),
            P("sec", None, exp + ("hid",)),
            P("sec", exp + ("hid",), None),
        ),
        out_specs=P(exp, ("sec", "hid")),
        check_vma=False,
    )
```

```python
import jax
import jax.numpy as jnp
from jax import lax
from jax.experimental import pallas as pl
from jax.experimental.pallas import tpu as pltpu
from jax.sharding import Mesh, PartitionSpec as P


EXPERTS = 8
MOST = 4
HID = 8
F32 = jnp.float32
BF16 = jnp.bfloat16

GROUP = ("group",)
SQUARE = ("sec", "xlo")


def prep_kernel(x_ref, out_ref, y_ref, sems):
    n, rows, w = x_ref.shape
    rows -= 8
    copies = out_ref.shape[0]
    total = jnp.zeros((rows, w), F32)
    for z in range(n):
        x = x_ref[z, 0:rows, :].astype(F32)
        g = x_ref[z, rows : rows + 1, :].astype(F32)
        total = total + x * x
        y_ref[z * rows : (z + 1) * rows, :] = (x * g).astype(BF16)
    col = jnp.sum(total, axis=1, keepdims=True)
    row = jnp.transpose(jnp.broadcast_to(col, (rows, rows)))[0:8, :]
    hi = row.astype(BF16).astype(F32)
    mid = (row - hi).astype(BF16).astype(F32)
    low = row - hi - mid
    which = lax.broadcasted_iota(jnp.int32, (8, rows), 0)
    parts = jnp.where(which == 0, hi, jnp.where(which == 1, mid, jnp.where(which == 2, low, 0.0)))
    y_ref[n * rows : n * rows + 8, :] = jnp.concatenate([parts, jnp.zeros((8, w - rows), F32)], axis=1).astype(BF16)
    sends = [pltpu.make_async_copy(y_ref, out_ref.at[j], sems.at[j]) for j in range(copies)]
    for send in sends:
        send.start()
    for send in sends:
        send.wait()


def gate_up_kernel(x_ref, g0, u0, g1, u1, act_ref, w_ref, acc_ref, sems):
    _, tall, w = x_ref.shape
    n = HID
    rows = (tall - 8) // n
    deep, ff = g0.shape
    chunks = 4
    per = deep // chunks
    loads = [
        [
            pltpu.make_async_copy(
                ref.at[c * per : (c + 1) * per, :], w_ref.at[i, c * per : (c + 1) * per, :], sems.at[c, i]
            )
            for i, ref in enumerate((g0, u0, g1, u1))
        ]
        for c in range(chunks)
    ]
    for group in loads:
        for load in group:
            load.start()
    scales = []
    for x in range(2):
        parts = [x_ref[2 * s + x, n * rows : n * rows + 8, 0:rows].astype(F32) for s in range(2)]
        both = parts[0] + parts[1]
        total = both[0:1, :] + both[1:2, :] + both[2:3, :]
        inv = 1.0 / jnp.sqrt(total / deep + 1e-05)
        scales.append(jnp.transpose(jnp.broadcast_to(inv, (rows, rows))))
    for c in range(chunks):
        pieces = range(c * per // w, (c + 1) * per // w)
        xs = jnp.concatenate(
            [
                jnp.concatenate(
                    [x_ref[2 * (p // n) + x, (p % n) * rows : (p % n + 1) * rows, :] for p in pieces], axis=1
                )
                for x in range(2)
            ],
            axis=0,
        )
        for load in loads[c]:
            load.wait()
        for k in range(2):
            ws = jnp.concatenate([w_ref[i, c * per : (c + 1) * per, :] for i in (2 * k, 2 * k + 1)], axis=1)
            part = jnp.dot(xs, ws, preferred_element_type=F32)
            if c == 0:
                acc_ref[k] = part
            else:
                acc_ref[k] += part
    for k in range(2):
        for x in range(2):
            block = acc_ref[k, x * rows : (x + 1) * rows, :]
            gate = block[:, 0:ff] * scales[x]
            up = block[:, ff:] * scales[x]
            act = (gate / (1.0 + jnp.exp(-gate)) * up).astype(BF16)
            for s in range(2):
                act_ref[2 * s + x, :, k * ff : (k + 1) * ff] = act


def down_kernel(act_ref, *refs):
    *downs, out_ref, w_ref, acc_ref, y_ref, sems, out_sems = refs
    n, _, w = out_ref.shape
    ff = downs[0].shape[0]
    loads = [pltpu.make_async_copy(ref, w_ref.at[i * ff : (i + 1) * ff], sems.at[i]) for i, ref in enumerate(downs)]
    for load in loads:
        load.start()
    place = lax.axis_index("sec") * 2 + lax.axis_index("xlo")
    sends = []
    for h in range(2):
        act = jnp.concatenate([act_ref[place ^ k] for k in (2 * h, 2 * h + 1)], axis=1)
        for load in loads[4 * h : 4 * h + 4]:
            load.wait()
        for z in range(n):
            part = jnp.dot(
                act, w_ref[4 * h * ff : 4 * (h + 1) * ff, z * w : (z + 1) * w], preferred_element_type=F32
            )
            if h == 0:
                acc_ref[z] = part
                continue
            y_ref[z] = (acc_ref[z] + part).astype(BF16)
            if z % 2:
                sends.append(
                    pltpu.make_async_copy(
                        y_ref.at[z - 1 : z + 1], out_ref.at[z - 1 : z + 1], out_sems.at[z // 2]
                    )
                )
                sends[-1].start()
    for send in sends:
        send.wait()


VM = pl.BlockSpec(memory_space=pltpu.VMEM)
HBM = pl.BlockSpec(memory_space=pltpu.HBM)


def vm(x):
    return pltpu.with_memory_space_constraint(x, pltpu.VMEM)


def hbm(x):
    return pltpu.with_memory_space_constraint(x, pltpu.HBM)


def prepared(x):
    n, rows, w = x.shape
    tall = n * (rows - 8) + 8
    return pl.pallas_call(
        prep_kernel,
        out_shape=pltpu.HBM((4, tall, w), BF16),
        in_specs=[VM],
        out_specs=HBM,
        scratch_shapes=[pltpu.VMEM((tall, w), BF16), pltpu.SemaphoreType.DMA((4,))],
        compiler_params=pltpu.CompilerParams(vmem_limit_bytes=4 << 20),
        name="prep",
    )(vm(x))


def gated(x, weights):
    _, tall, _ = x.shape
    rows = (tall - 8) // HID
    deep, ff = weights[0].shape
    return pl.pallas_call(
        gate_up_kernel,
        out_shape=pltpu.HBM((4, rows, 2 * ff), BF16),
        in_specs=[VM] + [HBM] * 4,
        out_specs=VM,
        scratch_shapes=[
            pltpu.VMEM((4, deep, ff), BF16),
            pltpu.VMEM((2, 2 * rows, 2 * ff), F32),
            pltpu.SemaphoreType.DMA((4, 4)),
        ],
        compiler_params=pltpu.CompilerParams(vmem_limit_bytes=16 << 20),
        name="gate_up",
    )(vm(x), *[hbm(v) for v in weights])


def lowered(act, downs):
    _, rows, _ = act.shape
    ff, wide = downs[0].shape
    shape = (HID, rows, wide // HID)
    return pl.pallas_call(
        down_kernel,
        out_shape=pltpu.HBM(shape, BF16),
        in_specs=[VM] + [HBM] * 8,
        out_specs=HBM,
        scratch_shapes=[
            pltpu.VMEM((8 * ff, wide), BF16),
            pltpu.VMEM(shape, F32),
            pltpu.VMEM(shape, BF16),
            pltpu.SemaphoreType.DMA((8,)),
            pltpu.SemaphoreType.DMA((HID // 2,)),
        ],
        compiler_params=pltpu.CompilerParams(vmem_limit_bytes=16 << 20),
        name="down",
    )(vm(act), *[hbm(v) for v in downs])


def exchange(x, axes):
    return lax.all_to_all(x, axes, split_axis=0, concat_axis=0, tiled=True)


def added(x):
    return jnp.sum(x.astype(F32), axis=0).astype(BF16)


def layer(tokens, norm_gain, route_weight, block_experts, w_gate, w_up, w_down):
    rows, w = tokens.shape
    groups = lax.axis_size("group")
    n_hid = lax.axis_size("hid")
    me = lax.axis_index("group")
    gate0, up0, down0 = w_gate[0], w_up[0], w_down[0]
    sec = lax.axis_index("sec")
    part = down0.shape[1] // 2
    down_away = lax.dynamic_slice_in_dim(down0, (1 - sec) * part, part, 1)

    def sent(x, flip):
        return lax.ppermute(x, SQUARE, [(i, i ^ flip) for i in range(4)])

    def swapped(x):
        return lax.ppermute(x, "core", [(0, 1), (1, 0)])

    away_x = sent(down_away, 3)
    gate1, up1 = swapped(gate0), swapped(up0)

    hit = jnp.any(block_experts == me, axis=1)
    slot_of_block = jnp.maximum(jnp.cumsum(hit.astype(jnp.int32)) - 1, 0)
    slot_ids = jnp.arange(MOST, dtype=jnp.int32)
    match = (slot_of_block[None, :] == slot_ids[:, None]) & hit[None, :]
    block_of_slot = jnp.sum(jnp.where(match, jnp.arange(groups, dtype=jnp.int32)[None, :], 0), axis=1)

    mine = jnp.take(block_experts, me, axis=0, mode="clip")
    named = mine[None, :] == jnp.arange(EXPERTS, dtype=jnp.int32)[:, None]
    factor = jnp.sum(jnp.where(named[:, None, :], route_weight[None], 0.0), axis=2)

    blocks = exchange(jnp.broadcast_to(tokens[None], (groups, rows, w)), GROUP)
    tall = MOST * rows
    picked = jnp.take(blocks, block_of_slot, axis=0, mode="clip").reshape(tall, w)
    picked, down_late = lax.optimization_barrier((picked, down0))
    down_here = lax.dynamic_slice_in_dim(down_late, sec * part, part, 1)
    direct = [down_here, sent(down_here, 1), sent(down_away, 2), away_x]
    downs = [d for piece in direct for d in (piece, swapped(piece))]
    picked = jnp.concatenate([picked, jnp.broadcast_to(norm_gain[None, :], (8, w))], axis=0)
    wide = exchange(jnp.broadcast_to(picked[None], (n_hid, tall + 8, w)), "hid")
    ready = prepared(wide)
    every = exchange(ready, SQUARE)
    act = exchange(gated(every, (gate0, up0, gate1, up1)), SQUARE)
    summed = added(exchange(lowered(act, downs), "hid")).reshape(MOST, rows, w)
    outgoing = jnp.take(summed, slot_of_block, axis=0, mode="clip")
    back = exchange(outgoing, GROUP)
    return jnp.sum(back.astype(F32) * factor[:, :, None], axis=0).astype(BF16)


def solution(mesh):
    devices = mesh.devices.reshape(2, EXPERTS, 2, 2, 8)
    fine = Mesh(devices, ("sec", "group", "xlo", "core", "hid"))
    exp = ("group", "xlo", "core")
    return jax.shard_map(
        layer,
        mesh=fine,
        in_specs=(
            P(exp, ("sec", "hid")),
            P(("sec", "hid")),
            P(exp, None),
            P(),
            P("sec", None, exp + ("hid",)),
            P("sec", None, exp + ("hid",)),
            P("sec", exp + ("hid",), None),
        ),
        out_specs=P(exp, ("sec", "hid")),
        check_vma=False,
    )
```

```python
import jax
import jax.numpy as jnp
from jax import lax
from jax.experimental import pallas as pl
from jax.experimental.pallas import tpu as pltpu
from jax.sharding import Mesh, PartitionSpec as P


EXPERTS = 8
MOST = 4
HID = 8
F32 = jnp.float32
BF16 = jnp.bfloat16

GROUP = ("group",)
SQUARE = ("sec", "xlo")


def prep_kernel(x_ref, y_ref):
    n, rows, w = x_ref.shape
    rows -= 8
    total = jnp.zeros((rows, w), F32)
    for z in range(n):
        x = x_ref[z, 0:rows, :].astype(F32)
        g = x_ref[z, rows : rows + 1, :].astype(F32)
        total = total + x * x
        y_ref[z * rows : (z + 1) * rows, :] = (x * g).astype(BF16)
    col = jnp.sum(total, axis=1, keepdims=True)
    row = jnp.transpose(jnp.broadcast_to(col, (rows, rows)))[0:8, :]
    hi = row.astype(BF16).astype(F32)
    mid = (row - hi).astype(BF16).astype(F32)
    low = row - hi - mid
    which = lax.broadcasted_iota(jnp.int32, (8, rows), 0)
    parts = jnp.where(which == 0, hi, jnp.where(which == 1, mid, jnp.where(which == 2, low, 0.0)))
    y_ref[n * rows : n * rows + 8, :] = jnp.concatenate([parts, jnp.zeros((8, w - rows), F32)], axis=1).astype(BF16)


def gate_up_kernel(own, far, one, two, g0, u0, g1, u1, act_ref, w_ref, acc_ref, mid_ref, sems, mid_sems):
    tall, w = own.shape
    n = HID
    rows = (tall - 8) // n
    deep, ff = g0.shape
    chunks = 4
    per = deep // chunks
    sec, xlo, core = lax.axis_index("sec"), lax.axis_index("xlo"), lax.axis_index("core")
    moves = [
        pltpu.make_async_copy(one, mid_ref.at[core], mid_sems.at[0]),
        pltpu.make_async_copy(two, mid_ref.at[1 - core], mid_sems.at[1]),
    ]
    for move in moves:
        move.start()

    def source(ref, c):
        return ref.at[pl.ds(pl.multiple_of((sec ^ (c // 2)) * (deep // 2) + (c % 2) * per, per), per), :]

    loads = [
        [
            pltpu.make_async_copy(source(ref, c), w_ref.at[i, c * per : (c + 1) * per, :], sems.at[c, i])
            for i, ref in enumerate((g0, u0, g1, u1))
        ]
        for c in range(chunks)
    ]
    for group in loads:
        for load in group:
            load.start()
    for move in moves:
        move.wait()
    pieces = ((own, mid_ref.at[0]), (mid_ref.at[1], far))
    scales = []
    for x in range(2):
        parts = [pieces[s][x][n * rows : n * rows + 8, 0:rows].astype(F32) for s in range(2)]
        both = parts[0] + parts[1]
        total = both[0:1, :] + both[1:2, :] + both[2:3, :]
        inv = 1.0 / jnp.sqrt(total / deep + 1e-05)
        scales.append(jnp.transpose(jnp.broadcast_to(inv, (rows, rows))))
    for c in range(chunks):
        first = c % 2 * per // w
        xs = jnp.concatenate(
            [
                jnp.concatenate(
                    [pieces[c // 2][x][z * rows : (z + 1) * rows, :] for z in range(first, first + per // w)], axis=1
                )
                for x in range(2)
            ],
            axis=0,
        )
        for load in loads[c]:
            load.wait()
        for k in range(2):
            ws = jnp.concatenate([w_ref[i, c * per : (c + 1) * per, :] for i in (2 * k, 2 * k + 1)], axis=1)
            part = jnp.dot(xs, ws, preferred_element_type=F32)
            if c == 0:
                acc_ref[k] = part
            else:
                acc_ref[k] += part
    for k in range(2):
        for x in range(2):
            block = acc_ref[k, x * rows : (x + 1) * rows, :]
            gate = block[:, 0:ff] * scales[x]
            up = block[:, ff:] * scales[x]
            act = (gate / (1.0 + jnp.exp(-gate)) * up).astype(BF16)
            for s in range(2):
                act_ref[2 * s + (xlo ^ x), :, k * ff : (k + 1) * ff] = act


def down_kernel(act_ref, *refs):
    *downs, out_ref, w_ref, acc_ref, y_ref, sems, out_sems = refs
    n, _, w = out_ref.shape
    ff = downs[0].shape[0]
    loads = [pltpu.make_async_copy(ref, w_ref.at[i * ff : (i + 1) * ff], sems.at[i]) for i, ref in enumerate(downs)]
    for load in loads:
        load.start()
    place = lax.axis_index("sec") * 2 + lax.axis_index("xlo")
    sends = []
    for h in range(2):
        act = jnp.concatenate([act_ref[place ^ k] for k in (2 * h, 2 * h + 1)], axis=1)
        for load in loads[4 * h : 4 * h + 4]:
            load.wait()
        for z in range(n):
            part = jnp.dot(
                act, w_ref[4 * h * ff : 4 * (h + 1) * ff, z * w : (z + 1) * w], preferred_element_type=F32
            )
            if h == 0:
                acc_ref[z] = part
                continue
            y_ref[z] = (acc_ref[z] + part).astype(BF16)
            if z % 2:
                sends.append(
                    pltpu.make_async_copy(
                        y_ref.at[z - 1 : z + 1], out_ref.at[z - 1 : z + 1], out_sems.at[z // 2]
                    )
                )
                sends[-1].start()
    for send in sends:
        send.wait()


VM = pl.BlockSpec(memory_space=pltpu.VMEM)
HBM = pl.BlockSpec(memory_space=pltpu.HBM)


def vm(x):
    return pltpu.with_memory_space_constraint(x, pltpu.VMEM)


def hbm(x):
    return pltpu.with_memory_space_constraint(x, pltpu.HBM)


def prepared(x):
    n, rows, w = x.shape
    return pl.pallas_call(
        prep_kernel,
        out_shape=jax.ShapeDtypeStruct((n * (rows - 8) + 8, w), BF16),
        in_specs=[VM],
        out_specs=VM,
        compiler_params=pltpu.CompilerParams(vmem_limit_bytes=4 << 20),
        name="prep",
    )(vm(x))


def gated(own, far, one, two, weights):
    tall, w = own.shape
    rows = (tall - 8) // HID
    deep, ff = weights[0].shape
    return pl.pallas_call(
        gate_up_kernel,
        out_shape=pltpu.HBM((4, rows, 2 * ff), BF16),
        in_specs=[VM] * 2 + [HBM] * 6,
        out_specs=VM,
        scratch_shapes=[
            pltpu.VMEM((4, deep, ff), BF16),
            pltpu.VMEM((2, 2 * rows, 2 * ff), F32),
            pltpu.VMEM((2, tall, w), BF16),
            pltpu.SemaphoreType.DMA((4, 4)),
            pltpu.SemaphoreType.DMA((2,)),
        ],
        compiler_params=pltpu.CompilerParams(vmem_limit_bytes=16 << 20),
        name="gate_up",
    )(vm(own), vm(far), *[hbm(v) for v in (one, two, *weights)])


def lowered(act, downs):
    _, rows, _ = act.shape
    ff, wide = downs[0].shape
    shape = (HID, rows, wide // HID)
    return pl.pallas_call(
        down_kernel,
        out_shape=pltpu.HBM(shape, BF16),
        in_specs=[VM] + [HBM] * 8,
        out_specs=HBM,
        scratch_shapes=[
            pltpu.VMEM((8 * ff, wide), BF16),
            pltpu.VMEM(shape, F32),
            pltpu.VMEM(shape, BF16),
            pltpu.SemaphoreType.DMA((8,)),
            pltpu.SemaphoreType.DMA((HID // 2,)),
        ],
        compiler_params=pltpu.CompilerParams(vmem_limit_bytes=16 << 20),
        name="down",
    )(vm(act), *[hbm(v) for v in downs])


def exchange(x, axes):
    return lax.all_to_all(x, axes, split_axis=0, concat_axis=0, tiled=True)


def added(x):
    return jnp.sum(x.astype(F32), axis=0).astype(BF16)


def turned(x, turn):
    devices = [(place, core) for place in range(4) for core in range(2)]
    pairs = [(p * 2 + c, (p ^ (1 if c == turn else 2)) * 2 + c) for p, c in devices]
    return lax.ppermute(x, (*SQUARE, "core"), pairs)


def layer(tokens, norm_gain, route_weight, block_experts, w_gate, w_up, w_down):
    rows, w = tokens.shape
    groups = lax.axis_size("group")
    n_hid = lax.axis_size("hid")
    me = lax.axis_index("group")
    gate0, up0, down0 = w_gate[0], w_up[0], w_down[0]
    sec = lax.axis_index("sec")
    part = down0.shape[1] // 2
    down_away = lax.dynamic_slice_in_dim(down0, (1 - sec) * part, part, 1)

    def sent(x, flip):
        return lax.ppermute(x, SQUARE, [(i, i ^ flip) for i in range(4)])

    def swapped(x):
        return lax.ppermute(x, "core", [(0, 1), (1, 0)])

    away_x = sent(down_away, 3)
    gate1, up1 = swapped(gate0), swapped(up0)

    hit = jnp.any(block_experts == me, axis=1)
    slot_of_block = jnp.maximum(jnp.cumsum(hit.astype(jnp.int32)) - 1, 0)
    slot_ids = jnp.arange(MOST, dtype=jnp.int32)
    match = (slot_of_block[None, :] == slot_ids[:, None]) & hit[None, :]
    block_of_slot = jnp.sum(jnp.where(match, jnp.arange(groups, dtype=jnp.int32)[None, :], 0), axis=1)

    mine = jnp.take(block_experts, me, axis=0, mode="clip")
    named = mine[None, :] == jnp.arange(EXPERTS, dtype=jnp.int32)[:, None]
    factor = jnp.sum(jnp.where(named[:, None, :], route_weight[None], 0.0), axis=2)

    blocks = exchange(jnp.broadcast_to(tokens[None], (groups, rows, w)), GROUP)
    tall = MOST * rows
    picked = jnp.take(blocks, block_of_slot, axis=0, mode="clip").reshape(tall, w)
    picked, down_late = lax.optimization_barrier((picked, down0))
    down_here = lax.dynamic_slice_in_dim(down_late, sec * part, part, 1)
    direct = [down_here, sent(down_here, 1), sent(down_away, 2), away_x]
    downs = [d for piece in direct for d in (piece, swapped(piece))]
    picked = jnp.concatenate([picked, jnp.broadcast_to(norm_gain[None, :], (8, w))], axis=0)
    wide = exchange(jnp.broadcast_to(picked[None], (n_hid, tall + 8, w)), "hid")
    own = prepared(wide)
    one = turned(own, 0)
    two = turned(own, 1)
    far = turned(one, 1)
    act = exchange(gated(own, far, one, two, (gate0, up0, gate1, up1)), SQUARE)
    summed = added(exchange(lowered(act, downs), "hid")).reshape(MOST, rows, w)
    outgoing = jnp.take(summed, slot_of_block, axis=0, mode="clip")
    back = exchange(outgoing, GROUP)
    return jnp.sum(back.astype(F32) * factor[:, :, None], axis=0).astype(BF16)


def solution(mesh):
    devices = mesh.devices.reshape(2, EXPERTS, 2, 2, 8)
    fine = Mesh(devices, ("sec", "group", "xlo", "core", "hid"))
    exp = ("group", "xlo", "core")
    return jax.shard_map(
        layer,
        mesh=fine,
        in_specs=(
            P(exp, ("sec", "hid")),
            P(("sec", "hid")),
            P(exp, None),
            P(),
            P("sec", None, exp + ("hid",)),
            P("sec", None, exp + ("hid",)),
            P("sec", exp + ("hid",), None),
        ),
        out_specs=P(exp, ("sec", "hid")),
        check_vma=False,
    )
```

```python
import jax
import jax.numpy as jnp
from jax import lax
from jax.experimental import pallas as pl
from jax.experimental.pallas import tpu as pltpu
from jax.sharding import Mesh, PartitionSpec as P


EXPERTS = 8
MOST = 4
HID = 8
F32 = jnp.float32
BF16 = jnp.bfloat16

GROUP = ("group",)
SQUARE = ("sec", "xlo")


def prep_kernel(x_ref, out_ref, y_ref, sems):
    n, rows, w = x_ref.shape
    rows -= 8
    copies = out_ref.shape[0]
    total = jnp.zeros((rows, w), F32)
    for z in range(n):
        x = x_ref[z, 0:rows, :].astype(F32)
        g = x_ref[z, rows : rows + 1, :].astype(F32)
        total = total + x * x
        y_ref[z * rows : (z + 1) * rows, :] = (x * g).astype(BF16)
    col = jnp.sum(total, axis=1, keepdims=True)
    row = jnp.transpose(jnp.broadcast_to(col, (rows, rows)))[0:8, :]
    hi = row.astype(BF16).astype(F32)
    mid = (row - hi).astype(BF16).astype(F32)
    low = row - hi - mid
    which = lax.broadcasted_iota(jnp.int32, (8, rows), 0)
    parts = jnp.where(which == 0, hi, jnp.where(which == 1, mid, jnp.where(which == 2, low, 0.0)))
    y_ref[n * rows : n * rows + 8, :] = jnp.concatenate([parts, jnp.zeros((8, w - rows), F32)], axis=1).astype(BF16)
    sends = [pltpu.make_async_copy(y_ref, out_ref.at[j], sems.at[j]) for j in range(copies)]
    for send in sends:
        send.start()
    for send in sends:
        send.wait()


def gate_up_kernel(x_ref, g0, u0, g1, u1, act_ref, w_ref, acc_ref, sems):
    _, tall, w = x_ref.shape
    n = HID
    rows = (tall - 8) // n
    deep, ff = g0.shape
    chunks = 4
    per = deep // chunks
    loads = [
        [
            pltpu.make_async_copy(
                ref.at[c * per : (c + 1) * per, :], w_ref.at[i, c * per : (c + 1) * per, :], sems.at[c, i]
            )
            for i, ref in enumerate((g0, u0, g1, u1))
        ]
        for c in range(chunks)
    ]
    for group in loads:
        for load in group:
            load.start()
    scales = []
    for x in range(2):
        parts = [x_ref[2 * s + x, n * rows : n * rows + 8, 0:rows].astype(F32) for s in range(2)]
        both = parts[0] + parts[1]
        total = both[0:1, :] + both[1:2, :] + both[2:3, :]
        inv = 1.0 / jnp.sqrt(total / deep + 1e-05)
        scales.append(jnp.transpose(jnp.broadcast_to(inv, (rows, rows))))
    for c in range(chunks):
        pieces = range(c * per // w, (c + 1) * per // w)
        xs = jnp.concatenate(
            [
                jnp.concatenate(
                    [x_ref[2 * (p // n) + x, (p % n) * rows : (p % n + 1) * rows, :] for p in pieces], axis=1
                )
                for x in range(2)
            ],
            axis=0,
        )
        for load in loads[c]:
            load.wait()
        for k in range(2):
            ws = jnp.concatenate([w_ref[i, c * per : (c + 1) * per, :] for i in (2 * k, 2 * k + 1)], axis=1)
            part = jnp.dot(xs, ws, preferred_element_type=F32)
            if c == 0:
                acc_ref[k] = part
            else:
                acc_ref[k] += part
    for k in range(2):
        for x in range(2):
            block = acc_ref[k, x * rows : (x + 1) * rows, :]
            gate = block[:, 0:ff] * scales[x]
            up = block[:, ff:] * scales[x]
            act = (gate / (1.0 + jnp.exp(-gate)) * up).astype(BF16)
            for s in range(2):
                act_ref[2 * s + x, :, k * ff : (k + 1) * ff] = act


def down_kernel(act_ref, *refs):
    *downs, out_ref, w_ref, acc_ref, y_ref, sems, out_sems = refs
    n, _, w = out_ref.shape
    ff = downs[0].shape[0]
    loads = [pltpu.make_async_copy(ref, w_ref.at[i * ff : (i + 1) * ff], sems.at[i]) for i, ref in enumerate(downs)]
    for load in loads:
        load.start()
    place = lax.axis_index("sec") * 2 + lax.axis_index("xlo")
    sends = []
    for h in range(2):
        act = jnp.concatenate([act_ref[place ^ k] for k in (2 * h, 2 * h + 1)], axis=1)
        for load in loads[4 * h : 4 * h + 4]:
            load.wait()
        for z in range(n):
            part = jnp.dot(
                act, w_ref[4 * h * ff : 4 * (h + 1) * ff, z * w : (z + 1) * w], preferred_element_type=F32
            )
            if h == 0:
                acc_ref[z] = part
                continue
            y_ref[z] = (acc_ref[z] + part).astype(BF16)
            if z % 2:
                sends.append(
                    pltpu.make_async_copy(
                        y_ref.at[z - 1 : z + 1], out_ref.at[z - 1 : z + 1], out_sems.at[z // 2]
                    )
                )
                sends[-1].start()
    for send in sends:
        send.wait()


def routed(experts_ref, me):
    count = jnp.int32(0)
    block_of_slot = [jnp.int32(0)] * MOST
    slot_of_block = []
    for b in range(experts_ref.shape[1]):
        hit = (experts_ref[0, b] == me) | (experts_ref[1, b] == me)
        block_of_slot = [jnp.where(hit & (count == k), b, old) for k, old in enumerate(block_of_slot)]
        slot_of_block.append(jnp.minimum(count, MOST - 1))
        count = count + jnp.where(hit, 1, 0)
    return block_of_slot, slot_of_block


def sent_all(sends):
    for send in sends:
        send.start()
    for send in sends:
        send.wait()


def pick_kernel(experts_ref, x_ref, gain_ref, out_ref, y_ref, sems):
    _, rows, w = x_ref.shape
    block_of_slot, _ = routed(experts_ref, lax.axis_index("group"))
    for k, block in enumerate(block_of_slot):
        y_ref[k * rows : (k + 1) * rows, :] = x_ref[block]
    y_ref[MOST * rows :, :] = jnp.broadcast_to(gain_ref[...].astype(F32), (8, w)).astype(BF16)
    sent_all([pltpu.make_async_copy(y_ref, out_ref.at[j], sems.at[j]) for j in range(out_ref.shape[0])])


def home_kernel(experts_ref, x_ref, out_ref, y_ref, sems):
    blocks, rows, _ = out_ref.shape
    _, slot_of_block = routed(experts_ref, lax.axis_index("group"))
    for k in range(MOST):
        total = x_ref[0, k * rows : (k + 1) * rows, :].astype(F32)
        for z in range(1, x_ref.shape[0]):
            total = total + x_ref[z, k * rows : (k + 1) * rows, :].astype(F32)
        y_ref[k] = total.astype(BF16)
    sent_all([pltpu.make_async_copy(y_ref.at[slot_of_block[b]], out_ref.at[b], sems.at[b]) for b in range(blocks)])


SM = pl.BlockSpec(memory_space=pltpu.SMEM)
VM = pl.BlockSpec(memory_space=pltpu.VMEM)
HBM = pl.BlockSpec(memory_space=pltpu.HBM)


def vm(x):
    return pltpu.with_memory_space_constraint(x, pltpu.VMEM)


def hbm(x):
    return pltpu.with_memory_space_constraint(x, pltpu.HBM)


def prepared(x):
    n, rows, w = x.shape
    tall = n * (rows - 8) + 8
    return pl.pallas_call(
        prep_kernel,
        out_shape=pltpu.HBM((4, tall, w), BF16),
        in_specs=[VM],
        out_specs=HBM,
        scratch_shapes=[pltpu.VMEM((tall, w), BF16), pltpu.SemaphoreType.DMA((4,))],
        compiler_params=pltpu.CompilerParams(vmem_limit_bytes=4 << 20),
        name="prep",
    )(vm(x))


def gated(x, weights):
    _, tall, _ = x.shape
    rows = (tall - 8) // HID
    deep, ff = weights[0].shape
    return pl.pallas_call(
        gate_up_kernel,
        out_shape=pltpu.HBM((4, rows, 2 * ff), BF16),
        in_specs=[VM] + [HBM] * 4,
        out_specs=VM,
        scratch_shapes=[
            pltpu.VMEM((4, deep, ff), BF16),
            pltpu.VMEM((2, 2 * rows, 2 * ff), F32),
            pltpu.SemaphoreType.DMA((4, 4)),
        ],
        compiler_params=pltpu.CompilerParams(vmem_limit_bytes=16 << 20),
        name="gate_up",
    )(vm(x), *[hbm(v) for v in weights])


def lowered(act, downs):
    _, rows, _ = act.shape
    ff, wide = downs[0].shape
    shape = (HID, rows, wide // HID)
    return pl.pallas_call(
        down_kernel,
        out_shape=pltpu.HBM(shape, BF16),
        in_specs=[VM] + [HBM] * 8,
        out_specs=HBM,
        scratch_shapes=[
            pltpu.VMEM((8 * ff, wide), BF16),
            pltpu.VMEM(shape, F32),
            pltpu.VMEM(shape, BF16),
            pltpu.SemaphoreType.DMA((8,)),
            pltpu.SemaphoreType.DMA((HID // 2,)),
        ],
        compiler_params=pltpu.CompilerParams(vmem_limit_bytes=16 << 20),
        name="down",
    )(vm(act), *[hbm(v) for v in downs])


def picked_rows(block_experts, blocks, norm_gain, copies):
    _, rows, w = blocks.shape
    tall = MOST * rows + 8
    return pl.pallas_call(
        pick_kernel,
        out_shape=pltpu.HBM((copies, tall, w), BF16),
        in_specs=[SM, VM, VM],
        out_specs=HBM,
        scratch_shapes=[pltpu.VMEM((tall, w), BF16), pltpu.SemaphoreType.DMA((copies,))],
        compiler_params=pltpu.CompilerParams(vmem_limit_bytes=1 << 20),
    )(block_experts.T, vm(blocks), norm_gain[None, :])


def homed(block_experts, parts):
    _, tall, w = parts.shape
    shape = (block_experts.shape[0], tall // MOST, w)
    return pl.pallas_call(
        home_kernel,
        out_shape=pltpu.HBM(shape, BF16),
        in_specs=[SM, VM],
        out_specs=HBM,
        scratch_shapes=[pltpu.VMEM((MOST, *shape[1:]), BF16), pltpu.SemaphoreType.DMA((shape[0],))],
        compiler_params=pltpu.CompilerParams(vmem_limit_bytes=2 << 20),
        name="home",
    )(block_experts.T, vm(parts))


def exchange(x, axes):
    return lax.all_to_all(x, axes, split_axis=0, concat_axis=0, tiled=True)


def layer(tokens, norm_gain, route_weight, block_experts, w_gate, w_up, w_down):
    rows, w = tokens.shape
    groups = lax.axis_size("group")
    n_hid = lax.axis_size("hid")
    gate0, up0, down0 = w_gate[0], w_up[0], w_down[0]
    sec = lax.axis_index("sec")
    part = down0.shape[1] // 2
    down_away = lax.dynamic_slice_in_dim(down0, (1 - sec) * part, part, 1)

    def sent(x, flip):
        return lax.ppermute(x, SQUARE, [(i, i ^ flip) for i in range(4)])

    def swapped(x):
        return lax.ppermute(x, "core", [(0, 1), (1, 0)])

    away_x = sent(down_away, 3)
    gate1, up1 = swapped(gate0), swapped(up0)

    mine = jnp.take(block_experts, lax.axis_index("group"), axis=0, mode="clip")
    named = mine[None, :] == jnp.arange(EXPERTS, dtype=jnp.int32)[:, None]
    factor = jnp.sum(jnp.where(named[:, None, :], route_weight[None], 0.0), axis=2)

    blocks = exchange(jnp.broadcast_to(tokens[None], (groups, rows, w)), GROUP)
    wide = picked_rows(block_experts, blocks, norm_gain, n_hid)
    blocks, down_late = lax.optimization_barrier((blocks, down0))
    down_here = lax.dynamic_slice_in_dim(down_late, sec * part, part, 1)
    direct = [down_here, sent(down_here, 1), sent(down_away, 2), away_x]
    downs = [d for piece in direct for d in (piece, swapped(piece))]
    wide = exchange(wide, "hid")
    ready = prepared(wide)
    every = exchange(ready, SQUARE)
    act = exchange(gated(every, (gate0, up0, gate1, up1)), SQUARE)
    back = exchange(homed(block_experts, exchange(lowered(act, downs), "hid")), GROUP)
    return jnp.sum(back.astype(F32) * factor[:, :, None], axis=0).astype(BF16)


def solution(mesh):
    devices = mesh.devices.reshape(2, EXPERTS, 2, 2, 8)
    fine = Mesh(devices, ("sec", "group", "xlo", "core", "hid"))
    exp = ("group", "xlo", "core")
    return jax.shard_map(
        layer,
        mesh=fine,
        in_specs=(
            P(exp, ("sec", "hid")),
            P(("sec", "hid")),
            P(exp, None),
            P(),
            P("sec", None, exp + ("hid",)),
            P("sec", None, exp + ("hid",)),
            P("sec", exp + ("hid",), None),
        ),
        out_specs=P(exp, ("sec", "hid")),
        check_vma=False,
    )
```

```python
import jax
import jax.numpy as jnp
from jax import lax
from jax.experimental import pallas as pl
from jax.experimental.pallas import tpu as pltpu
from jax.sharding import Mesh, PartitionSpec as P


EXPERTS = 8
MOST = 4
HID = 8
F32 = jnp.float32
BF16 = jnp.bfloat16

GROUP = ("group",)
SQUARE = ("sec", "xlo")


def prep_kernel(x_ref, out_ref, y_ref, sems):
    n, rows, w = x_ref.shape
    rows -= 8
    copies = out_ref.shape[0]
    total = jnp.zeros((rows, w), F32)
    for z in range(n):
        x = x_ref[z, 0:rows, :].astype(F32)
        g = x_ref[z, rows : rows + 1, :].astype(F32)
        total = total + x * x
        y_ref[z * rows : (z + 1) * rows, :] = (x * g).astype(BF16)
    col = jnp.sum(total, axis=1, keepdims=True)
    row = jnp.transpose(jnp.broadcast_to(col, (rows, rows)))[0:8, :]
    hi = row.astype(BF16).astype(F32)
    mid = (row - hi).astype(BF16).astype(F32)
    low = row - hi - mid
    which = lax.broadcasted_iota(jnp.int32, (8, rows), 0)
    parts = jnp.where(which == 0, hi, jnp.where(which == 1, mid, jnp.where(which == 2, low, 0.0)))
    y_ref[n * rows : n * rows + 8, :] = jnp.concatenate([parts, jnp.zeros((8, w - rows), F32)], axis=1).astype(BF16)
    sends = [pltpu.make_async_copy(y_ref, out_ref.at[j], sems.at[j]) for j in range(copies)]
    for send in sends:
        send.start()
    for send in sends:
        send.wait()


def gate_up_kernel(x_ref, g0, u0, g1, u1, act_ref, w_ref, acc_ref, sems):
    _, tall, w = x_ref.shape
    n = HID
    rows = (tall - 8) // n
    deep, ff = g0.shape
    chunks = 4
    per = deep // chunks
    loads = [
        [
            pltpu.make_async_copy(
                ref.at[c * per : (c + 1) * per, :], w_ref.at[i, c * per : (c + 1) * per, :], sems.at[c, i]
            )
            for i, ref in enumerate((g0, u0, g1, u1))
        ]
        for c in range(chunks)
    ]
    for group in loads:
        for load in group:
            load.start()
    scales = []
    for x in range(2):
        parts = [x_ref[2 * s + x, n * rows : n * rows + 8, 0:rows].astype(F32) for s in range(2)]
        both = parts[0] + parts[1]
        total = both[0:1, :] + both[1:2, :] + both[2:3, :]
        inv = 1.0 / jnp.sqrt(total / deep + 1e-05)
        scales.append(jnp.transpose(jnp.broadcast_to(inv, (rows, rows))))
    for c in range(chunks):
        pieces = range(c * per // w, (c + 1) * per // w)
        xs = jnp.concatenate(
            [
                jnp.concatenate(
                    [x_ref[2 * (p // n) + x, (p % n) * rows : (p % n + 1) * rows, :] for p in pieces], axis=1
                )
                for x in range(2)
            ],
            axis=0,
        )
        for load in loads[c]:
            load.wait()
        for k in range(2):
            ws = jnp.concatenate([w_ref[i, c * per : (c + 1) * per, :] for i in (2 * k, 2 * k + 1)], axis=1)
            part = jnp.dot(xs, ws, preferred_element_type=F32)
            if c == 0:
                acc_ref[k] = part
            else:
                acc_ref[k] += part
    for k in range(2):
        for x in range(2):
            block = acc_ref[k, x * rows : (x + 1) * rows, :]
            gate = block[:, 0:ff] * scales[x]
            up = block[:, ff:] * scales[x]
            act = (gate / (1.0 + jnp.exp(-gate)) * up).astype(BF16)
            for s in range(2):
                act_ref[2 * s + x, :, k * ff : (k + 1) * ff] = act


def down_kernel(act_ref, *refs):
    *downs, out_ref, w_ref, acc_ref, y_ref, sems, out_sems = refs
    n, _, w = out_ref.shape
    ff = downs[0].shape[0]
    loads = [pltpu.make_async_copy(ref, w_ref.at[i * ff : (i + 1) * ff], sems.at[i]) for i, ref in enumerate(downs)]
    for load in loads:
        load.start()
    place = lax.axis_index("sec") * 2 + lax.axis_index("xlo")
    sends = []
    for h in range(2):
        act = jnp.concatenate([act_ref[place ^ k] for k in (2 * h, 2 * h + 1)], axis=1)
        for load in loads[4 * h : 4 * h + 4]:
            load.wait()
        for z in range(n):
            part = jnp.dot(
                act, w_ref[4 * h * ff : 4 * (h + 1) * ff, z * w : (z + 1) * w], preferred_element_type=F32
            )
            if h == 0:
                acc_ref[z] = part
                continue
            y_ref[z] = (acc_ref[z] + part).astype(BF16)
            if z % 2:
                sends.append(
                    pltpu.make_async_copy(
                        y_ref.at[z - 1 : z + 1], out_ref.at[z - 1 : z + 1], out_sems.at[z // 2]
                    )
                )
                sends[-1].start()
    for send in sends:
        send.wait()


def routed(experts_ref, me):
    count = jnp.int32(0)
    block_of_slot = [jnp.int32(0)] * MOST
    slot_of_block = []
    for b in range(experts_ref.shape[1]):
        hit = (experts_ref[0, b] == me) | (experts_ref[1, b] == me)
        block_of_slot = [jnp.where(hit & (count == k), b, old) for k, old in enumerate(block_of_slot)]
        slot_of_block.append(jnp.minimum(count, MOST - 1))
        count = count + jnp.where(hit, 1, 0)
    return block_of_slot, slot_of_block


def sent_all(sends):
    for send in sends:
        send.start()
    for send in sends:
        send.wait()


def pick_kernel(experts_hbm, x_ref, gain_hbm, out_ref, y_ref, experts_ref, gain_ref, sems):
    _, rows, w = x_ref.shape
    loads = [
        pltpu.make_async_copy(experts_hbm, experts_ref, sems.at[out_ref.shape[0]]),
        pltpu.make_async_copy(gain_hbm, gain_ref, sems.at[out_ref.shape[0] + 1]),
    ]
    sent_all(loads)
    y_ref[MOST * rows :, :] = jnp.broadcast_to(gain_ref[...].astype(F32)[None, :], (8, w)).astype(BF16)
    block_of_slot, _ = routed(experts_ref, lax.axis_index("group"))
    for k, block in enumerate(block_of_slot):
        y_ref[k * rows : (k + 1) * rows, :] = x_ref[block]
    sent_all([pltpu.make_async_copy(y_ref, out_ref.at[j], sems.at[j]) for j in range(out_ref.shape[0])])


def home_kernel(experts_ref, x_ref, out_ref, y_ref, sems):
    blocks, rows, _ = out_ref.shape
    _, slot_of_block = routed(experts_ref, lax.axis_index("group"))
    for k in range(MOST):
        total = x_ref[0, k * rows : (k + 1) * rows, :].astype(F32)
        for z in range(1, x_ref.shape[0]):
            total = total + x_ref[z, k * rows : (k + 1) * rows, :].astype(F32)
        y_ref[k] = total.astype(BF16)
    sent_all([pltpu.make_async_copy(y_ref.at[slot_of_block[b]], out_ref.at[b], sems.at[b]) for b in range(blocks)])


SM = pl.BlockSpec(memory_space=pltpu.SMEM)
VM = pl.BlockSpec(memory_space=pltpu.VMEM)
HBM = pl.BlockSpec(memory_space=pltpu.HBM)


def vm(x):
    return pltpu.with_memory_space_constraint(x, pltpu.VMEM)


def hbm(x):
    return pltpu.with_memory_space_constraint(x, pltpu.HBM)


def prepared(x):
    n, rows, w = x.shape
    tall = n * (rows - 8) + 8
    return pl.pallas_call(
        prep_kernel,
        out_shape=pltpu.HBM((4, tall, w), BF16),
        in_specs=[VM],
        out_specs=HBM,
        scratch_shapes=[pltpu.VMEM((tall, w), BF16), pltpu.SemaphoreType.DMA((4,))],
        compiler_params=pltpu.CompilerParams(vmem_limit_bytes=4 << 20),
        name="prep",
    )(vm(x))


def gated(x, weights):
    _, tall, _ = x.shape
    rows = (tall - 8) // HID
    deep, ff = weights[0].shape
    return pl.pallas_call(
        gate_up_kernel,
        out_shape=pltpu.HBM((4, rows, 2 * ff), BF16),
        in_specs=[VM] + [HBM] * 4,
        out_specs=VM,
        scratch_shapes=[
            pltpu.VMEM((4, deep, ff), BF16),
            pltpu.VMEM((2, 2 * rows, 2 * ff), F32),
            pltpu.SemaphoreType.DMA((4, 4)),
        ],
        compiler_params=pltpu.CompilerParams(vmem_limit_bytes=16 << 20),
        name="gate_up",
    )(vm(x), *[hbm(v) for v in weights])


def lowered(act, downs):
    _, rows, _ = act.shape
    ff, wide = downs[0].shape
    shape = (HID, rows, wide // HID)
    return pl.pallas_call(
        down_kernel,
        out_shape=pltpu.HBM(shape, BF16),
        in_specs=[VM] + [HBM] * 8,
        out_specs=HBM,
        scratch_shapes=[
            pltpu.VMEM((8 * ff, wide), BF16),
            pltpu.VMEM(shape, F32),
            pltpu.VMEM(shape, BF16),
            pltpu.SemaphoreType.DMA((8,)),
            pltpu.SemaphoreType.DMA((HID // 2,)),
        ],
        compiler_params=pltpu.CompilerParams(vmem_limit_bytes=16 << 20),
        name="down",
    )(vm(act), *[hbm(v) for v in downs])


def picked_rows(block_experts, blocks, norm_gain, copies):
    _, rows, w = blocks.shape
    tall = MOST * rows + 8
    return pl.pallas_call(
        pick_kernel,
        out_shape=pltpu.HBM((copies, tall, w), BF16),
        in_specs=[HBM, VM, HBM],
        out_specs=HBM,
        scratch_shapes=[
            pltpu.VMEM((tall, w), BF16),
            pltpu.SMEM(block_experts.shape[::-1], jnp.int32),
            pltpu.VMEM((w,), BF16),
            pltpu.SemaphoreType.DMA((copies + 2,)),
        ],
        compiler_params=pltpu.CompilerParams(vmem_limit_bytes=1 << 20),
    )(hbm(block_experts.T), vm(blocks), hbm(norm_gain))


def homed(block_experts, parts):
    _, tall, w = parts.shape
    shape = (block_experts.shape[0], tall // MOST, w)
    return pl.pallas_call(
        home_kernel,
        out_shape=pltpu.HBM(shape, BF16),
        in_specs=[SM, VM],
        out_specs=HBM,
        scratch_shapes=[pltpu.VMEM((MOST, *shape[1:]), BF16), pltpu.SemaphoreType.DMA((shape[0],))],
        compiler_params=pltpu.CompilerParams(vmem_limit_bytes=2 << 20),
        name="home",
    )(block_experts.T, vm(parts))


def exchange(x, axes):
    return lax.all_to_all(x, axes, split_axis=0, concat_axis=0, tiled=True)


def layer(tokens, norm_gain, route_weight, block_experts, w_gate, w_up, w_down):
    rows, w = tokens.shape
    groups = lax.axis_size("group")
    n_hid = lax.axis_size("hid")
    gate0, up0, down0 = w_gate[0], w_up[0], w_down[0]
    sec = lax.axis_index("sec")
    part = down0.shape[1] // 2
    down_away = lax.dynamic_slice_in_dim(down0, (1 - sec) * part, part, 1)

    def sent(x, flip):
        return lax.ppermute(x, SQUARE, [(i, i ^ flip) for i in range(4)])

    def swapped(x):
        return lax.ppermute(x, "core", [(0, 1), (1, 0)])

    away_x = sent(down_away, 3)
    gate1, up1 = swapped(gate0), swapped(up0)

    mine = jnp.take(block_experts, lax.axis_index("group"), axis=0, mode="clip")
    named = mine[None, :] == jnp.arange(EXPERTS, dtype=jnp.int32)[:, None]
    factor = jnp.sum(jnp.where(named[:, None, :], route_weight[None], 0.0), axis=2)

    blocks = exchange(jnp.broadcast_to(tokens[None], (groups, rows, w)), GROUP)
    wide = picked_rows(block_experts, blocks, norm_gain, n_hid)
    blocks, down_late = lax.optimization_barrier((blocks, down0))
    down_here = lax.dynamic_slice_in_dim(down_late, sec * part, part, 1)
    direct = [down_here, sent(down_here, 1), sent(down_away, 2), away_x]
    downs = [d for piece in direct for d in (piece, swapped(piece))]
    wide = exchange(wide, "hid")
    ready = prepared(wide)
    every = exchange(ready, SQUARE)
    act = exchange(gated(every, (gate0, up0, gate1, up1)), SQUARE)
    back = exchange(homed(block_experts, exchange(lowered(act, downs), "hid")), GROUP)
    return jnp.sum(back.astype(F32) * factor[:, :, None], axis=0).astype(BF16)


def solution(mesh):
    devices = mesh.devices.reshape(2, EXPERTS, 2, 2, 8)
    fine = Mesh(devices, ("sec", "group", "xlo", "core", "hid"))
    exp = ("group", "xlo", "core")
    return jax.shard_map(
        layer,
        mesh=fine,
        in_specs=(
            P(exp, ("sec", "hid")),
            P(("sec", "hid")),
            P(exp, None),
            P(),
            P("sec", None, exp + ("hid",)),
            P("sec", None, exp + ("hid",)),
            P("sec", exp + ("hid",), None),
        ),
        out_specs=P(exp, ("sec", "hid")),
        check_vma=False,
    )
```

```python
import jax
import jax.numpy as jnp
from jax import lax
from jax.experimental import pallas as pl
from jax.experimental.pallas import tpu as pltpu
from jax.sharding import Mesh, PartitionSpec as P


EXPERTS = 8
MOST = 4
HID = 8
F32 = jnp.float32
BF16 = jnp.bfloat16

GROUP = ("group",)
SQUARE = ("sec", "xlo")


def place_of(z):
    return (z + 1) % HID


def prep_kernel(x_ref, out_ref, y_ref, sems):
    n, rows, w = x_ref.shape
    rows -= 8
    copies = out_ref.shape[0]
    total = jnp.zeros((rows, w), F32)
    for z in range(n):
        k = place_of(z)
        x = x_ref[k, 0:rows, :].astype(F32)
        g = x_ref[k, rows : rows + 1, :].astype(F32)
        total = total + x * x
        y_ref[z * rows : (z + 1) * rows, :] = (x * g).astype(BF16)
    col = jnp.sum(total, axis=1, keepdims=True)
    row = jnp.transpose(jnp.broadcast_to(col, (rows, rows)))[0:8, :]
    hi = row.astype(BF16).astype(F32)
    mid = (row - hi).astype(BF16).astype(F32)
    low = row - hi - mid
    which = lax.broadcasted_iota(jnp.int32, (8, rows), 0)
    parts = jnp.where(which == 0, hi, jnp.where(which == 1, mid, jnp.where(which == 2, low, 0.0)))
    y_ref[n * rows : n * rows + 8, :] = jnp.concatenate([parts, jnp.zeros((8, w - rows), F32)], axis=1).astype(BF16)
    sends = [pltpu.make_async_copy(y_ref, out_ref.at[j], sems.at[j]) for j in range(copies)]
    for send in sends:
        send.start()
    for send in sends:
        send.wait()


def gate_up_kernel(x_ref, g0, u0, g1, u1, act_ref, w_ref, acc_ref, sems):
    _, tall, w = x_ref.shape
    n = HID
    rows = (tall - 8) // n
    deep, ff = g0.shape
    chunks = 4
    per = deep // chunks
    loads = [
        [
            pltpu.make_async_copy(
                ref.at[c * per : (c + 1) * per, :], w_ref.at[i, c * per : (c + 1) * per, :], sems.at[c, i]
            )
            for i, ref in enumerate((g0, u0, g1, u1))
        ]
        for c in range(chunks)
    ]
    for group in loads:
        for load in group:
            load.start()
    scales = []
    for x in range(2):
        parts = [x_ref[2 * s + x, n * rows : n * rows + 8, 0:rows].astype(F32) for s in range(2)]
        both = parts[0] + parts[1]
        total = both[0:1, :] + both[1:2, :] + both[2:3, :]
        inv = 1.0 / jnp.sqrt(total / deep + 1e-05)
        scales.append(jnp.transpose(jnp.broadcast_to(inv, (rows, rows))))
    for c in range(chunks):
        pieces = range(c * per // w, (c + 1) * per // w)
        xs = jnp.concatenate(
            [
                jnp.concatenate(
                    [x_ref[2 * (p // n) + x, (p % n) * rows : (p % n + 1) * rows, :] for p in pieces], axis=1
                )
                for x in range(2)
            ],
            axis=0,
        )
        for load in loads[c]:
            load.wait()
        for k in range(2):
            ws = jnp.concatenate([w_ref[i, c * per : (c + 1) * per, :] for i in (2 * k, 2 * k + 1)], axis=1)
            part = jnp.dot(xs, ws, preferred_element_type=F32)
            if c == 0:
                acc_ref[k] = part
            else:
                acc_ref[k] += part
    for k in range(2):
        for x in range(2):
            block = acc_ref[k, x * rows : (x + 1) * rows, :]
            gate = block[:, 0:ff] * scales[x]
            up = block[:, ff:] * scales[x]
            act = (gate / (1.0 + jnp.exp(-gate)) * up).astype(BF16)
            for s in range(2):
                act_ref[2 * s + x, :, k * ff : (k + 1) * ff] = act


def down_kernel(act_ref, *refs):
    *downs, out_ref, w_ref, acc_ref, y_ref, sems, out_sems = refs
    n, _, w = out_ref.shape
    ff = downs[0].shape[0]
    loads = [pltpu.make_async_copy(ref, w_ref.at[i * ff : (i + 1) * ff], sems.at[i]) for i, ref in enumerate(downs)]
    for load in loads:
        load.start()
    place = lax.axis_index("sec") * 2 + lax.axis_index("xlo")
    sends = []
    for h in range(2):
        act = jnp.concatenate([act_ref[place ^ k] for k in (2 * h, 2 * h + 1)], axis=1)
        for load in loads[4 * h : 4 * h + 4]:
            load.wait()
        for z in range(n):
            part = jnp.dot(
                act, w_ref[4 * h * ff : 4 * (h + 1) * ff, z * w : (z + 1) * w], preferred_element_type=F32
            )
            if h == 0:
                acc_ref[z] = part
                continue
            k = place_of(z)
            y_ref[k] = (acc_ref[z] + part).astype(BF16)
            sends.append(pltpu.make_async_copy(y_ref.at[k], out_ref.at[k], out_sems.at[k]))
            sends[-1].start()
    for send in sends:
        send.wait()


def routed(experts_ref, me):
    count = jnp.int32(0)
    block_of_slot = [jnp.int32(0)] * MOST
    slot_of_block = []
    for b in range(experts_ref.shape[1]):
        hit = (experts_ref[0, b] == me) | (experts_ref[1, b] == me)
        block_of_slot = [jnp.where(hit & (count == k), b, old) for k, old in enumerate(block_of_slot)]
        slot_of_block.append(jnp.minimum(count, MOST - 1))
        count = count + jnp.where(hit, 1, 0)
    return block_of_slot, slot_of_block


def sent_all(sends):
    for send in sends:
        send.start()
    for send in sends:
        send.wait()


def pick_kernel(experts_hbm, x_ref, gain_hbm, out_ref, y_ref, experts_ref, gain_ref, sems):
    _, rows, w = x_ref.shape
    loads = [
        pltpu.make_async_copy(experts_hbm, experts_ref, sems.at[out_ref.shape[0]]),
        pltpu.make_async_copy(gain_hbm, gain_ref, sems.at[out_ref.shape[0] + 1]),
    ]
    sent_all(loads)
    y_ref[MOST * rows :, :] = jnp.broadcast_to(gain_ref[...].astype(F32)[None, :], (8, w)).astype(BF16)
    block_of_slot, _ = routed(experts_ref, lax.axis_index("group"))
    for k, block in enumerate(block_of_slot):
        y_ref[k * rows : (k + 1) * rows, :] = x_ref[block]
    sent_all([pltpu.make_async_copy(y_ref, out_ref.at[j], sems.at[j]) for j in range(out_ref.shape[0])])


def home_kernel(experts_ref, x_ref, out_ref, y_ref, sems):
    blocks, rows, _ = out_ref.shape
    _, slot_of_block = routed(experts_ref, lax.axis_index("group"))
    for k in range(MOST):
        total = x_ref[0, k * rows : (k + 1) * rows, :].astype(F32)
        for z in range(1, x_ref.shape[0]):
            total = total + x_ref[z, k * rows : (k + 1) * rows, :].astype(F32)
        y_ref[k] = total.astype(BF16)
    sent_all([pltpu.make_async_copy(y_ref.at[slot_of_block[b]], out_ref.at[b], sems.at[b]) for b in range(blocks)])


SM = pl.BlockSpec(memory_space=pltpu.SMEM)
VM = pl.BlockSpec(memory_space=pltpu.VMEM)
HBM = pl.BlockSpec(memory_space=pltpu.HBM)


def vm(x):
    return pltpu.with_memory_space_constraint(x, pltpu.VMEM)


def hbm(x):
    return pltpu.with_memory_space_constraint(x, pltpu.HBM)


def prepared(x):
    n, rows, w = x.shape
    tall = n * (rows - 8) + 8
    return pl.pallas_call(
        prep_kernel,
        out_shape=pltpu.HBM((4, tall, w), BF16),
        in_specs=[VM],
        out_specs=HBM,
        scratch_shapes=[pltpu.VMEM((tall, w), BF16), pltpu.SemaphoreType.DMA((4,))],
        compiler_params=pltpu.CompilerParams(vmem_limit_bytes=4 << 20),
        name="prep",
    )(vm(x))


def gated(x, weights):
    _, tall, _ = x.shape
    rows = (tall - 8) // HID
    deep, ff = weights[0].shape
    return pl.pallas_call(
        gate_up_kernel,
        out_shape=pltpu.HBM((4, rows, 2 * ff), BF16),
        in_specs=[VM] + [HBM] * 4,
        out_specs=VM,
        scratch_shapes=[
            pltpu.VMEM((4, deep, ff), BF16),
            pltpu.VMEM((2, 2 * rows, 2 * ff), F32),
            pltpu.SemaphoreType.DMA((4, 4)),
        ],
        compiler_params=pltpu.CompilerParams(vmem_limit_bytes=16 << 20),
        name="gate_up",
    )(vm(x), *[hbm(v) for v in weights])


def lowered(act, downs):
    _, rows, _ = act.shape
    ff, wide = downs[0].shape
    shape = (HID, rows, wide // HID)
    return pl.pallas_call(
        down_kernel,
        out_shape=pltpu.HBM(shape, BF16),
        in_specs=[VM] + [HBM] * 8,
        out_specs=HBM,
        scratch_shapes=[
            pltpu.VMEM((8 * ff, wide), BF16),
            pltpu.VMEM(shape, F32),
            pltpu.VMEM(shape, BF16),
            pltpu.SemaphoreType.DMA((8,)),
            pltpu.SemaphoreType.DMA((HID,)),
        ],
        compiler_params=pltpu.CompilerParams(vmem_limit_bytes=16 << 20),
        name="down",
    )(vm(act), *[hbm(v) for v in downs])


def picked_rows(block_experts, blocks, norm_gain, copies):
    _, rows, w = blocks.shape
    tall = MOST * rows + 8
    return pl.pallas_call(
        pick_kernel,
        out_shape=pltpu.HBM((copies, tall, w), BF16),
        in_specs=[HBM, VM, HBM],
        out_specs=HBM,
        scratch_shapes=[
            pltpu.VMEM((tall, w), BF16),
            pltpu.SMEM(block_experts.shape[::-1], jnp.int32),
            pltpu.VMEM((w,), BF16),
            pltpu.SemaphoreType.DMA((copies + 2,)),
        ],
        compiler_params=pltpu.CompilerParams(vmem_limit_bytes=1 << 20),
    )(hbm(block_experts.T), vm(blocks), hbm(norm_gain))


def homed(block_experts, parts):
    _, tall, w = parts.shape
    shape = (block_experts.shape[0], tall // MOST, w)
    return pl.pallas_call(
        home_kernel,
        out_shape=pltpu.HBM(shape, BF16),
        in_specs=[SM, VM],
        out_specs=HBM,
        scratch_shapes=[pltpu.VMEM((MOST, *shape[1:]), BF16), pltpu.SemaphoreType.DMA((shape[0],))],
        compiler_params=pltpu.CompilerParams(vmem_limit_bytes=2 << 20),
        name="home",
    )(block_experts.T, vm(parts))


def exchange(x, axes, listing=None):
    return lax.all_to_all(x, axes, split_axis=0, concat_axis=0, axis_index_groups=listing, tiled=True)


COLUMN = [sorted(range(HID), key=place_of)]


def layer(tokens, norm_gain, route_weight, block_experts, w_gate, w_up, w_down):
    rows, w = tokens.shape
    groups = lax.axis_size("group")
    n_hid = lax.axis_size("hid")
    gate0, up0, down0 = w_gate[0], w_up[0], w_down[0]
    sec = lax.axis_index("sec")
    part = down0.shape[1] // 2
    down_away = lax.dynamic_slice_in_dim(down0, (1 - sec) * part, part, 1)

    def sent(x, flip):
        return lax.ppermute(x, SQUARE, [(i, i ^ flip) for i in range(4)])

    def swapped(x):
        return lax.ppermute(x, "core", [(0, 1), (1, 0)])

    away_x = sent(down_away, 3)
    gate1, up1 = swapped(gate0), swapped(up0)

    mine = jnp.take(block_experts, lax.axis_index("group"), axis=0, mode="clip")
    named = mine[None, :] == jnp.arange(EXPERTS, dtype=jnp.int32)[:, None]
    factor = jnp.sum(jnp.where(named[:, None, :], route_weight[None], 0.0), axis=2)

    blocks = exchange(jnp.broadcast_to(tokens[None], (groups, rows, w)), GROUP)
    wide = picked_rows(block_experts, blocks, norm_gain, n_hid)
    blocks, down_late = lax.optimization_barrier((blocks, down0))
    down_here = lax.dynamic_slice_in_dim(down_late, sec * part, part, 1)
    direct = [down_here, sent(down_here, 1), sent(down_away, 2), away_x]
    downs = [d for piece in direct for d in (piece, swapped(piece))]
    wide = exchange(wide, "hid", COLUMN)
    ready = prepared(wide)
    every = exchange(ready, SQUARE)
    act = exchange(gated(every, (gate0, up0, gate1, up1)), SQUARE)
    back = exchange(homed(block_experts, exchange(lowered(act, downs), "hid", COLUMN)), GROUP)
    return jnp.sum(back.astype(F32) * factor[:, :, None], axis=0).astype(BF16)


def solution(mesh):
    devices = mesh.devices.reshape(2, EXPERTS, 2, 2, 8)
    fine = Mesh(devices, ("sec", "group", "xlo", "core", "hid"))
    exp = ("group", "xlo", "core")
    return jax.shard_map(
        layer,
        mesh=fine,
        in_specs=(
            P(exp, ("sec", "hid")),
            P(("sec", "hid")),
            P(exp, None),
            P(),
            P("sec", None, exp + ("hid",)),
            P("sec", None, exp + ("hid",)),
            P("sec", exp + ("hid",), None),
        ),
        out_specs=P(exp, ("sec", "hid")),
        check_vma=False,
    )
```

```python
import jax
import jax.numpy as jnp
from jax import lax
from jax.experimental import pallas as pl
from jax.experimental.pallas import tpu as pltpu
from jax.sharding import Mesh, PartitionSpec as P


EXPERTS = 8
MOST = 4
HID = 8
F32 = jnp.float32
BF16 = jnp.bfloat16

FAR = 5
GROUP = "group"
SQUARE = ("sec", "xlo")


def place_of(z):
    return (z + 1) % HID


def prep_kernel(x_ref, out_ref, y_ref, sems):
    n, rows, w = x_ref.shape
    rows -= 8
    copies = out_ref.shape[0]
    total = jnp.zeros((rows, w), F32)
    for z in range(n):
        k = place_of(z)
        x = x_ref[k, 0:rows, :].astype(F32)
        g = x_ref[k, rows : rows + 1, :].astype(F32)
        total = total + x * x
        y_ref[z * rows : (z + 1) * rows, :] = (x * g).astype(BF16)
    col = jnp.sum(total, axis=1, keepdims=True)
    row = jnp.transpose(jnp.broadcast_to(col, (rows, rows)))[0:8, :]
    hi = row.astype(BF16).astype(F32)
    mid = (row - hi).astype(BF16).astype(F32)
    low = row - hi - mid
    which = lax.broadcasted_iota(jnp.int32, (8, rows), 0)
    parts = jnp.where(which == 0, hi, jnp.where(which == 1, mid, jnp.where(which == 2, low, 0.0)))
    y_ref[n * rows : n * rows + 8, :] = jnp.concatenate([parts, jnp.zeros((8, w - rows), F32)], axis=1).astype(BF16)
    sends = [pltpu.make_async_copy(y_ref, out_ref.at[j], sems.at[j]) for j in range(copies)]
    for send in sends:
        send.start()
    for send in sends:
        send.wait()


def gate_up_kernel(x_ref, g0, u0, g1, u1, act_ref, w_ref, acc_ref, sems):
    _, tall, w = x_ref.shape
    n = HID
    rows = (tall - 8) // n
    deep, ff = g0.shape
    chunks = 4
    per = deep // chunks
    loads = [
        [
            pltpu.make_async_copy(
                ref.at[c * per : (c + 1) * per, :], w_ref.at[i, c * per : (c + 1) * per, :], sems.at[c, i]
            )
            for i, ref in enumerate((g0, u0, g1, u1))
        ]
        for c in range(chunks)
    ]
    for group in loads:
        for load in group:
            load.start()
    scales = []
    for x in range(2):
        parts = [x_ref[2 * s + x, n * rows : n * rows + 8, 0:rows].astype(F32) for s in range(2)]
        both = parts[0] + parts[1]
        total = both[0:1, :] + both[1:2, :] + both[2:3, :]
        inv = 1.0 / jnp.sqrt(total / deep + 1e-05)
        scales.append(jnp.transpose(jnp.broadcast_to(inv, (rows, rows))))
    for c in range(chunks):
        pieces = range(c * per // w, (c + 1) * per // w)
        xs = jnp.concatenate(
            [
                jnp.concatenate(
                    [x_ref[2 * (p // n) + x, (p % n) * rows : (p % n + 1) * rows, :] for p in pieces], axis=1
                )
                for x in range(2)
            ],
            axis=0,
        )
        for load in loads[c]:
            load.wait()
        for k in range(2):
            ws = jnp.concatenate([w_ref[i, c * per : (c + 1) * per, :] for i in (2 * k, 2 * k + 1)], axis=1)
            part = jnp.dot(xs, ws, preferred_element_type=F32)
            if c == 0:
                acc_ref[k] = part
            else:
                acc_ref[k] += part
    for k in range(2):
        for x in range(2):
            block = acc_ref[k, x * rows : (x + 1) * rows, :]
            gate = block[:, 0:ff] * scales[x]
            up = block[:, ff:] * scales[x]
            act = (gate / (1.0 + jnp.exp(-gate)) * up).astype(BF16)
            for s in range(2):
                act_ref[2 * s + x, :, k * ff : (k + 1) * ff] = act


def down_kernel(act_ref, *refs):
    *downs, out_ref, w_ref, acc_ref, y_ref, sems, out_sems = refs
    n, _, w = out_ref.shape
    ff = downs[0].shape[0]
    loads = [pltpu.make_async_copy(ref, w_ref.at[i * ff : (i + 1) * ff], sems.at[i]) for i, ref in enumerate(downs)]
    for load in loads:
        load.start()
    place = lax.axis_index("sec") * 2 + lax.axis_index("xlo")
    sends = []
    for h in range(2):
        act = jnp.concatenate([act_ref[place ^ k] for k in (2 * h, 2 * h + 1)], axis=1)
        for load in loads[4 * h : 4 * h + 4]:
            load.wait()
        for z in range(n):
            part = jnp.dot(
                act, w_ref[4 * h * ff : 4 * (h + 1) * ff, z * w : (z + 1) * w], preferred_element_type=F32
            )
            if h == 0:
                acc_ref[z] = part
                continue
            k = place_of(z)
            y_ref[k] = (acc_ref[z] + part).astype(BF16)
            sends.append(pltpu.make_async_copy(y_ref.at[k], out_ref.at[k], out_sems.at[k]))
            sends[-1].start()
    for send in sends:
        send.wait()


def routed(experts_ref, me):
    count = jnp.int32(0)
    block_of_slot = [jnp.int32(0)] * MOST
    slot_of_block = []
    for b in range(experts_ref.shape[1]):
        hit = (experts_ref[0, b] == me) | (experts_ref[1, b] == me)
        block_of_slot = [jnp.where(hit & (count == k), b, old) for k, old in enumerate(block_of_slot)]
        slot_of_block.append(jnp.minimum(count, MOST - 1))
        count = count + jnp.where(hit, 1, 0)
    return block_of_slot, slot_of_block


def sent_all(sends):
    for send in sends:
        send.start()
    for send in sends:
        send.wait()


def pick_kernel(experts_hbm, x_ref, gain_hbm, out_ref, y_ref, experts_ref, gain_ref, sems):
    _, rows, w = x_ref.shape
    loads = [
        pltpu.make_async_copy(experts_hbm, experts_ref, sems.at[out_ref.shape[0]]),
        pltpu.make_async_copy(gain_hbm, gain_ref, sems.at[out_ref.shape[0] + 1]),
    ]
    sent_all(loads)
    y_ref[MOST * rows :, :] = jnp.broadcast_to(gain_ref[...].astype(F32)[None, :], (8, w)).astype(BF16)
    block_of_slot, _ = routed(experts_ref, lax.axis_index("group"))
    for k, block in enumerate(block_of_slot):
        y_ref[k * rows : (k + 1) * rows, :] = x_ref[block ^ FAR]
    sent_all([pltpu.make_async_copy(y_ref, out_ref.at[j], sems.at[j]) for j in range(out_ref.shape[0])])


def home_kernel(experts_ref, x_ref, out_ref, y_ref, sems):
    blocks, rows, _ = out_ref.shape
    _, slot_of_block = routed(experts_ref, lax.axis_index("group"))
    for k in range(MOST):
        total = x_ref[0, k * rows : (k + 1) * rows, :].astype(F32)
        for z in range(1, x_ref.shape[0]):
            total = total + x_ref[z, k * rows : (k + 1) * rows, :].astype(F32)
        y_ref[k] = total.astype(BF16)
    sent_all(
        [pltpu.make_async_copy(y_ref.at[slot_of_block[b]], out_ref.at[b ^ FAR], sems.at[b]) for b in range(blocks)]
    )


SM = pl.BlockSpec(memory_space=pltpu.SMEM)
VM = pl.BlockSpec(memory_space=pltpu.VMEM)
HBM = pl.BlockSpec(memory_space=pltpu.HBM)


def vm(x):
    return pltpu.with_memory_space_constraint(x, pltpu.VMEM)


def hbm(x):
    return pltpu.with_memory_space_constraint(x, pltpu.HBM)


def prepared(x):
    n, rows, w = x.shape
    tall = n * (rows - 8) + 8
    return pl.pallas_call(
        prep_kernel,
        out_shape=pltpu.HBM((4, tall, w), BF16),
        in_specs=[VM],
        out_specs=HBM,
        scratch_shapes=[pltpu.VMEM((tall, w), BF16), pltpu.SemaphoreType.DMA((4,))],
        compiler_params=pltpu.CompilerParams(vmem_limit_bytes=4 << 20),
        name="prep",
    )(vm(x))


def gated(x, weights):
    _, tall, _ = x.shape
    rows = (tall - 8) // HID
    deep, ff = weights[0].shape
    return pl.pallas_call(
        gate_up_kernel,
        out_shape=pltpu.HBM((4, rows, 2 * ff), BF16),
        in_specs=[VM] + [HBM] * 4,
        out_specs=VM,
        scratch_shapes=[
            pltpu.VMEM((4, deep, ff), BF16),
            pltpu.VMEM((2, 2 * rows, 2 * ff), F32),
            pltpu.SemaphoreType.DMA((4, 4)),
        ],
        compiler_params=pltpu.CompilerParams(vmem_limit_bytes=16 << 20),
        name="gate_up",
    )(vm(x), *[hbm(v) for v in weights])


def lowered(act, downs):
    _, rows, _ = act.shape
    ff, wide = downs[0].shape
    shape = (HID, rows, wide // HID)
    return pl.pallas_call(
        down_kernel,
        out_shape=pltpu.HBM(shape, BF16),
        in_specs=[VM] + [HBM] * 8,
        out_specs=HBM,
        scratch_shapes=[
            pltpu.VMEM((8 * ff, wide), BF16),
            pltpu.VMEM(shape, F32),
            pltpu.VMEM(shape, BF16),
            pltpu.SemaphoreType.DMA((8,)),
            pltpu.SemaphoreType.DMA((HID,)),
        ],
        compiler_params=pltpu.CompilerParams(vmem_limit_bytes=16 << 20),
        name="down",
    )(vm(act), *[hbm(v) for v in downs])


def picked_rows(block_experts, blocks, norm_gain, copies):
    _, rows, w = blocks.shape
    tall = MOST * rows + 8
    return pl.pallas_call(
        pick_kernel,
        out_shape=pltpu.HBM((copies, tall, w), BF16),
        in_specs=[HBM, VM, HBM],
        out_specs=HBM,
        scratch_shapes=[
            pltpu.VMEM((tall, w), BF16),
            pltpu.SMEM(block_experts.shape[::-1], jnp.int32),
            pltpu.VMEM((w,), BF16),
            pltpu.SemaphoreType.DMA((copies + 2,)),
        ],
        compiler_params=pltpu.CompilerParams(vmem_limit_bytes=1 << 20),
    )(hbm(block_experts.T), vm(blocks), hbm(norm_gain))


def homed(block_experts, parts):
    _, tall, w = parts.shape
    shape = (block_experts.shape[0], tall // MOST, w)
    return pl.pallas_call(
        home_kernel,
        out_shape=pltpu.HBM(shape, BF16),
        in_specs=[SM, VM],
        out_specs=HBM,
        scratch_shapes=[pltpu.VMEM((MOST, *shape[1:]), BF16), pltpu.SemaphoreType.DMA((shape[0],))],
        compiler_params=pltpu.CompilerParams(vmem_limit_bytes=2 << 20),
        name="home",
    )(block_experts.T, vm(parts))


def exchange(x, axes, listing=None):
    return lax.all_to_all(x, axes, split_axis=0, concat_axis=0, axis_index_groups=listing, tiled=True)


ACROSS = [[g ^ FAR for g in range(EXPERTS)]]
COLUMN = [sorted(range(HID), key=place_of)]


def layer(tokens, norm_gain, route_weight, block_experts, w_gate, w_up, w_down):
    rows, w = tokens.shape
    groups = lax.axis_size("group")
    n_hid = lax.axis_size("hid")
    gate0, up0, down0 = w_gate[0], w_up[0], w_down[0]
    sec = lax.axis_index("sec")
    part = down0.shape[1] // 2
    down_away = lax.dynamic_slice_in_dim(down0, (1 - sec) * part, part, 1)

    def sent(x, flip):
        return lax.ppermute(x, SQUARE, [(i, i ^ flip) for i in range(4)])

    def swapped(x):
        return lax.ppermute(x, "core", [(0, 1), (1, 0)])

    away_x = sent(down_away, 3)
    gate1, up1 = swapped(gate0), swapped(up0)

    mine = jnp.take(block_experts, lax.axis_index("group"), axis=0, mode="clip")
    named = mine[None, :] == (jnp.arange(EXPERTS, dtype=jnp.int32) ^ FAR)[:, None]
    factor = jnp.sum(jnp.where(named[:, None, :], route_weight[None], 0.0), axis=2)

    blocks = exchange(jnp.broadcast_to(tokens[None], (groups, rows, w)), GROUP, ACROSS)
    wide = picked_rows(block_experts, blocks, norm_gain, n_hid)
    blocks, down_late = lax.optimization_barrier((blocks, down0))
    down_here = lax.dynamic_slice_in_dim(down_late, sec * part, part, 1)
    direct = [down_here, sent(down_here, 1), sent(down_away, 2), away_x]
    downs = [d for piece in direct for d in (piece, swapped(piece))]
    wide = exchange(wide, "hid", COLUMN)
    ready = prepared(wide)
    every = exchange(ready, SQUARE)
    act = exchange(gated(every, (gate0, up0, gate1, up1)), SQUARE)
    back = exchange(homed(block_experts, exchange(lowered(act, downs), "hid", COLUMN)), GROUP, ACROSS)
    return jnp.sum(back.astype(F32) * factor[:, :, None], axis=0).astype(BF16)


def solution(mesh):
    devices = mesh.devices.reshape(2, EXPERTS, 2, 2, 8)
    fine = Mesh(devices, ("sec", "group", "xlo", "core", "hid"))
    exp = ("group", "xlo", "core")
    return jax.shard_map(
        layer,
        mesh=fine,
        in_specs=(
            P(exp, ("sec", "hid")),
            P(("sec", "hid")),
            P(exp, None),
            P(),
            P("sec", None, exp + ("hid",)),
            P("sec", None, exp + ("hid",)),
            P("sec", exp + ("hid",), None),
        ),
        out_specs=P(exp, ("sec", "hid")),
        check_vma=False,
    )
```

```python
import jax
import jax.numpy as jnp
from jax import lax
from jax.experimental import pallas as pl
from jax.experimental.pallas import tpu as pltpu
from jax.sharding import Mesh, PartitionSpec as P


EXPERTS = 8
MOST = 4
HID = 8
F32 = jnp.float32
BF16 = jnp.bfloat16

FAR = 5
GROUP = "group"
SQUARE = ("sec", "xlo")


def place_of(z):
    return (z + 1) % HID


def prep_kernel(x_ref, out_ref, y_ref, sems):
    n, rows, w = x_ref.shape
    rows -= 8
    copies = out_ref.shape[0]
    total = jnp.zeros((rows, w), F32)
    for z in range(n):
        k = place_of(z)
        x = x_ref[k, 0:rows, :].astype(F32)
        g = x_ref[k, rows : rows + 1, :].astype(F32)
        total = total + x * x
        y_ref[z * rows : (z + 1) * rows, :] = (x * g).astype(BF16)
    col = jnp.sum(total, axis=1, keepdims=True)
    row = jnp.transpose(jnp.broadcast_to(col, (rows, rows)))[0:8, :]
    hi = row.astype(BF16).astype(F32)
    mid = (row - hi).astype(BF16).astype(F32)
    low = row - hi - mid
    which = lax.broadcasted_iota(jnp.int32, (8, rows), 0)
    parts = jnp.where(which == 0, hi, jnp.where(which == 1, mid, jnp.where(which == 2, low, 0.0)))
    y_ref[n * rows : n * rows + 8, :] = jnp.concatenate([parts, jnp.zeros((8, w - rows), F32)], axis=1).astype(BF16)
    sends = [pltpu.make_async_copy(y_ref, out_ref.at[j], sems.at[j]) for j in range(copies)]
    for send in sends:
        send.start()
    for send in sends:
        send.wait()


def gate_up_kernel(x_ref, g0, u0, g1, u1, act_ref, w_ref, acc_ref, sems):
    _, tall, w = x_ref.shape
    n = HID
    rows = (tall - 8) // n
    deep, ff = g0.shape
    chunks = 4
    per = deep // chunks
    loads = [
        [
            pltpu.make_async_copy(
                ref.at[c * per : (c + 1) * per, :], w_ref.at[i, c * per : (c + 1) * per, :], sems.at[c, i]
            )
            for i, ref in enumerate((g0, u0, g1, u1))
        ]
        for c in range(chunks)
    ]
    for group in loads:
        for load in group:
            load.start()
    scales = []
    for x in range(2):
        parts = [x_ref[3 - 2 * s - x, n * rows : n * rows + 8, 0:rows].astype(F32) for s in range(2)]
        both = parts[0] + parts[1]
        total = both[0:1, :] + both[1:2, :] + both[2:3, :]
        inv = 1.0 / jnp.sqrt(total / deep + 1e-05)
        scales.append(jnp.transpose(jnp.broadcast_to(inv, (rows, rows))))
    for c in range(chunks):
        pieces = range(c * per // w, (c + 1) * per // w)
        xs = jnp.concatenate(
            [
                jnp.concatenate(
                    [x_ref[3 - 2 * (p // n) - x, (p % n) * rows : (p % n + 1) * rows, :] for p in pieces], axis=1
                )
                for x in range(2)
            ],
            axis=0,
        )
        for load in loads[c]:
            load.wait()
        for k in range(2):
            ws = jnp.concatenate([w_ref[i, c * per : (c + 1) * per, :] for i in (2 * k, 2 * k + 1)], axis=1)
            part = jnp.dot(xs, ws, preferred_element_type=F32)
            if c == 0:
                acc_ref[k] = part
            else:
                acc_ref[k] += part
    for k in range(2):
        for x in range(2):
            block = acc_ref[k, x * rows : (x + 1) * rows, :]
            gate = block[:, 0:ff] * scales[x]
            up = block[:, ff:] * scales[x]
            act = (gate / (1.0 + jnp.exp(-gate)) * up).astype(BF16)
            for s in range(2):
                act_ref[3 - 2 * s - x, :, k * ff : (k + 1) * ff] = act


def down_kernel(act_ref, *refs):
    *downs, out_ref, w_ref, acc_ref, y_ref, sems, out_sems = refs
    n, _, w = out_ref.shape
    ff = downs[0].shape[0]
    loads = [pltpu.make_async_copy(ref, w_ref.at[i * ff : (i + 1) * ff], sems.at[i]) for i, ref in enumerate(downs)]
    for load in loads:
        load.start()
    place = lax.axis_index("sec") * 2 + lax.axis_index("xlo")
    sends = []
    for h in range(2):
        act = jnp.concatenate([act_ref[3 - (place ^ k)] for k in (2 * h, 2 * h + 1)], axis=1)
        for load in loads[4 * h : 4 * h + 4]:
            load.wait()
        for z in range(n):
            part = jnp.dot(
                act, w_ref[4 * h * ff : 4 * (h + 1) * ff, z * w : (z + 1) * w], preferred_element_type=F32
            )
            if h == 0:
                acc_ref[z] = part
                continue
            k = place_of(z)
            y_ref[k] = (acc_ref[z] + part).astype(BF16)
            sends.append(pltpu.make_async_copy(y_ref.at[k], out_ref.at[k], out_sems.at[k]))
            sends[-1].start()
    for send in sends:
        send.wait()


def routed(experts_ref, me):
    count = jnp.int32(0)
    block_of_slot = [jnp.int32(0)] * MOST
    slot_of_block = []
    for b in range(experts_ref.shape[1]):
        hit = (experts_ref[0, b] == me) | (experts_ref[1, b] == me)
        block_of_slot = [jnp.where(hit & (count == k), b, old) for k, old in enumerate(block_of_slot)]
        slot_of_block.append(jnp.minimum(count, MOST - 1))
        count = count + jnp.where(hit, 1, 0)
    return block_of_slot, slot_of_block


def sent_all(sends):
    for send in sends:
        send.start()
    for send in sends:
        send.wait()


def pick_kernel(experts_hbm, x_ref, gain_hbm, out_ref, y_ref, experts_ref, gain_ref, sems):
    _, rows, w = x_ref.shape
    loads = [
        pltpu.make_async_copy(experts_hbm, experts_ref, sems.at[out_ref.shape[0]]),
        pltpu.make_async_copy(gain_hbm, gain_ref, sems.at[out_ref.shape[0] + 1]),
    ]
    sent_all(loads)
    y_ref[MOST * rows :, :] = jnp.broadcast_to(gain_ref[...].astype(F32)[None, :], (8, w)).astype(BF16)
    block_of_slot, _ = routed(experts_ref, lax.axis_index("group"))
    for k, block in enumerate(block_of_slot):
        y_ref[k * rows : (k + 1) * rows, :] = x_ref[block ^ FAR]
    sent_all([pltpu.make_async_copy(y_ref, out_ref.at[j], sems.at[j]) for j in range(out_ref.shape[0])])


def home_kernel(experts_ref, x_ref, out_ref, y_ref, sems):
    blocks, rows, _ = out_ref.shape
    _, slot_of_block = routed(experts_ref, lax.axis_index("group"))
    for k in range(MOST):
        total = x_ref[0, k * rows : (k + 1) * rows, :].astype(F32)
        for z in range(1, x_ref.shape[0]):
            total = total + x_ref[z, k * rows : (k + 1) * rows, :].astype(F32)
        y_ref[k] = total.astype(BF16)
    sent_all(
        [pltpu.make_async_copy(y_ref.at[slot_of_block[b]], out_ref.at[b ^ FAR], sems.at[b]) for b in range(blocks)]
    )


SM = pl.BlockSpec(memory_space=pltpu.SMEM)
VM = pl.BlockSpec(memory_space=pltpu.VMEM)
HBM = pl.BlockSpec(memory_space=pltpu.HBM)


def vm(x):
    return pltpu.with_memory_space_constraint(x, pltpu.VMEM)


def hbm(x):
    return pltpu.with_memory_space_constraint(x, pltpu.HBM)


def prepared(x):
    n, rows, w = x.shape
    tall = n * (rows - 8) + 8
    return pl.pallas_call(
        prep_kernel,
        out_shape=pltpu.HBM((4, tall, w), BF16),
        in_specs=[VM],
        out_specs=HBM,
        scratch_shapes=[pltpu.VMEM((tall, w), BF16), pltpu.SemaphoreType.DMA((4,))],
        compiler_params=pltpu.CompilerParams(vmem_limit_bytes=4 << 20),
        name="prep",
    )(vm(x))


def gated(x, weights):
    _, tall, _ = x.shape
    rows = (tall - 8) // HID
    deep, ff = weights[0].shape
    return pl.pallas_call(
        gate_up_kernel,
        out_shape=pltpu.HBM((4, rows, 2 * ff), BF16),
        in_specs=[VM] + [HBM] * 4,
        out_specs=VM,
        scratch_shapes=[
            pltpu.VMEM((4, deep, ff), BF16),
            pltpu.VMEM((2, 2 * rows, 2 * ff), F32),
            pltpu.SemaphoreType.DMA((4, 4)),
        ],
        compiler_params=pltpu.CompilerParams(vmem_limit_bytes=16 << 20),
        name="gate_up",
    )(vm(x), *[hbm(v) for v in weights])


def lowered(act, downs):
    _, rows, _ = act.shape
    ff, wide = downs[0].shape
    shape = (HID, rows, wide // HID)
    return pl.pallas_call(
        down_kernel,
        out_shape=pltpu.HBM(shape, BF16),
        in_specs=[VM] + [HBM] * 8,
        out_specs=HBM,
        scratch_shapes=[
            pltpu.VMEM((8 * ff, wide), BF16),
            pltpu.VMEM(shape, F32),
            pltpu.VMEM(shape, BF16),
            pltpu.SemaphoreType.DMA((8,)),
            pltpu.SemaphoreType.DMA((HID,)),
        ],
        compiler_params=pltpu.CompilerParams(vmem_limit_bytes=16 << 20),
        name="down",
    )(vm(act), *[hbm(v) for v in downs])


def picked_rows(block_experts, blocks, norm_gain, copies):
    _, rows, w = blocks.shape
    tall = MOST * rows + 8
    return pl.pallas_call(
        pick_kernel,
        out_shape=pltpu.HBM((copies, tall, w), BF16),
        in_specs=[HBM, VM, HBM],
        out_specs=HBM,
        scratch_shapes=[
            pltpu.VMEM((tall, w), BF16),
            pltpu.SMEM(block_experts.shape[::-1], jnp.int32),
            pltpu.VMEM((w,), BF16),
            pltpu.SemaphoreType.DMA((copies + 2,)),
        ],
        compiler_params=pltpu.CompilerParams(vmem_limit_bytes=1 << 20),
    )(hbm(block_experts.T), vm(blocks), hbm(norm_gain))


def homed(block_experts, parts):
    _, tall, w = parts.shape
    shape = (block_experts.shape[0], tall // MOST, w)
    return pl.pallas_call(
        home_kernel,
        out_shape=pltpu.HBM(shape, BF16),
        in_specs=[SM, VM],
        out_specs=HBM,
        scratch_shapes=[pltpu.VMEM((MOST, *shape[1:]), BF16), pltpu.SemaphoreType.DMA((shape[0],))],
        compiler_params=pltpu.CompilerParams(vmem_limit_bytes=2 << 20),
        name="home",
    )(block_experts.T, vm(parts))


def exchange(x, axes, listing=None):
    return lax.all_to_all(x, axes, split_axis=0, concat_axis=0, axis_index_groups=listing, tiled=True)


ACROSS = [[g ^ FAR for g in range(EXPERTS)]]
CORNERS = [[3, 2, 1, 0]]
COLUMN = [sorted(range(HID), key=place_of)]


def layer(tokens, norm_gain, route_weight, block_experts, w_gate, w_up, w_down):
    rows, w = tokens.shape
    groups = lax.axis_size("group")
    n_hid = lax.axis_size("hid")
    gate0, up0, down0 = w_gate[0], w_up[0], w_down[0]
    sec = lax.axis_index("sec")
    part = down0.shape[1] // 2
    down_away = lax.dynamic_slice_in_dim(down0, (1 - sec) * part, part, 1)

    def sent(x, flip):
        return lax.ppermute(x, SQUARE, [(i, i ^ flip) for i in range(4)])

    def swapped(x):
        return lax.ppermute(x, "core", [(0, 1), (1, 0)])

    away_x = sent(down_away, 3)
    gate1, up1 = swapped(gate0), swapped(up0)

    mine = jnp.take(block_experts, lax.axis_index("group"), axis=0, mode="clip")
    named = mine[None, :] == (jnp.arange(EXPERTS, dtype=jnp.int32) ^ FAR)[:, None]
    factor = jnp.sum(jnp.where(named[:, None, :], route_weight[None], 0.0), axis=2)

    blocks = exchange(jnp.broadcast_to(tokens[None], (groups, rows, w)), GROUP, ACROSS)
    wide = picked_rows(block_experts, blocks, norm_gain, n_hid)
    blocks, down_late = lax.optimization_barrier((blocks, down0))
    down_here = lax.dynamic_slice_in_dim(down_late, sec * part, part, 1)
    direct = [down_here, sent(down_here, 1), sent(down_away, 2), away_x]
    downs = [d for piece in direct for d in (piece, swapped(piece))]
    wide = exchange(wide, "hid", COLUMN)
    ready = prepared(wide)
    every = exchange(ready, SQUARE, CORNERS)
    act = exchange(gated(every, (gate0, up0, gate1, up1)), SQUARE, CORNERS)
    back = exchange(homed(block_experts, exchange(lowered(act, downs), "hid", COLUMN)), GROUP, ACROSS)
    return jnp.sum(back.astype(F32) * factor[:, :, None], axis=0).astype(BF16)


def solution(mesh):
    devices = mesh.devices.reshape(2, EXPERTS, 2, 2, 8)
    fine = Mesh(devices, ("sec", "group", "xlo", "core", "hid"))
    exp = ("group", "xlo", "core")
    return jax.shard_map(
        layer,
        mesh=fine,
        in_specs=(
            P(exp, ("sec", "hid")),
            P(("sec", "hid")),
            P(exp, None),
            P(),
            P("sec", None, exp + ("hid",)),
            P("sec", None, exp + ("hid",)),
            P("sec", exp + ("hid",), None),
        ),
        out_specs=P(exp, ("sec", "hid")),
        check_vma=False,
    )
```
